256 devices in a mesh: cls: 8 (over x_hi, y), ptl: 32 (over x_lo, z, core).
Axes of the slice: x: 4 (x_hi: 2, x_lo: 2; x = x_hi * 2 + x_lo), y: 4, z: 8, core: 2. Of those that a mesh axis runs over, the one named last changes fastest.
Arguments:
- references: bfloat16 [8, 256, 4096], P('cls', 'ptl')
- particles: bfloat16 [131072, 4096], P(('cls', 'ptl'))
- class_ids: int32 [131072], P(('cls', 'ptl')), may hold values from 0 to 7, as said below
- orient_ids: int32 [131072], P(('cls', 'ptl')), may hold values from 0 to 255
- offsets: int32 [131072], P(('cls', 'ptl')), may hold values from -3 to 3
- weights: float32 [131072], P(('cls', 'ptl'))
Outputs:
- class_sums: float32 [8, 4096], P('cls', 'ptl')
The draws below stay inside these ranges and needn't reach their ends.
Inputs may be any that keep to these rules, and one draw needn't show every extreme that they name: `class_ids`: every class is the class of some particle; populations are uneven.
All inputs are finite; a program needn't handle non-finite values.
Results may differ from the reference program's by a relative error of at most 0.0028.
Values may be sent and summed in bfloat16 or wider, within the bound.
No kernel may reach another device: no remote copies, remote signals or barrier semaphores. Data moves between devices by JAX's collectives and lax.ppermute only.
A program may use at most 64 MiB of HBM per device.

```python
import math
import jax
import jax.numpy as jnp
from jax import lax

NX = 64
NY = 64
ORI = 256
SHIFT = 3
CLASSES = 8
PARTICLES = 131072


def helper_refs(key):
    return jax.random.normal(jax.random.fold_in(key, 11), (CLASSES, ORI, NX * NY), jnp.float32)


def helper_classes(key):
    base = jax.random.fold_in(key, 12)
    first = jax.random.randint(jax.random.fold_in(base, 1), (PARTICLES,), 0, CLASSES)
    second = jax.random.randint(jax.random.fold_in(base, 2), (PARTICLES,), 0, CLASSES)
    order = jax.random.permutation(jax.random.fold_in(base, 3), CLASSES)
    return order[(first + 1) * second // CLASSES].astype(jnp.int32)


def helper_orients(key):
    return jax.random.randint(jax.random.fold_in(key, 13), (PARTICLES,), 0, ORI).astype(jnp.int32)


def draw_references(key, part):
    return helper_refs(key).astype(jnp.bfloat16)


def draw_class_ids(key, part):
    return helper_classes(key)


def draw_orient_ids(key, part):
    return helper_orients(key)


def draw_particles(key, part):
    voxels = NX * NY
    values = jax.random.normal(jax.random.fold_in(key, 14), (PARTICLES, voxels), jnp.float32)
    return values.astype(jnp.bfloat16)


def draw_weights(key, part):
    lows = jnp.log(jnp.float32(0.2))
    values = jnp.exp(jax.random.uniform(jax.random.fold_in(key, 18), (PARTICLES,), jnp.float32, lows, 0.0))
    return values


def plant(values, rng, smallest, largest):
    index_at = [jax.random.randint(jax.random.fold_in(rng, axis), (), 0, length) for axis, length in enumerate(values.shape)]
    widest = values.shape.index(max(values.shape))
    beside = index_at[:widest] + [(index_at[widest] + 1) % values.shape[widest]] + index_at[widest + 1:]
    return values.at[tuple(index_at)].set(smallest).at[tuple(beside)].set(largest)


def setup_inputs(seed: int = 0) -> dict:
    streams_of = jax.random.split(jax.random.key(seed), 7)
    references = draw_references(jax.random.fold_in(streams_of[6], 71), 0)
    particles = draw_particles(jax.random.fold_in(streams_of[6], 71), 0)
    class_ids = draw_class_ids(jax.random.fold_in(streams_of[6], 71), 0)
    orient_ids = draw_orient_ids(jax.random.fold_in(streams_of[6], 71), 0)
    offsets = plant(jax.random.randint(streams_of[4], (PARTICLES,), 0 - SHIFT, SHIFT + 1), jax.random.fold_in(streams_of[4], 1), 0 - SHIFT, SHIFT).astype(jnp.int32)
    weights = draw_weights(jax.random.fold_in(streams_of[6], 71), 0)
    return {"references": references, "particles": particles, "class_ids": class_ids, "orient_ids": orient_ids, "offsets": offsets, "weights": weights}


def reference(references, particles, class_ids, orient_ids, offsets, weights):
    classes, orients, voxels = references.shape
    rows = references.reshape(classes * orients, voxels)
    count = particles.shape[0]
    block = math.gcd(count, 1024)
    scale = 1.0 / math.sqrt(voxels)
    flat_ids = (class_ids * orients + orient_ids).astype(jnp.int32)

    def block_scores(args):
        part, picks = args
        scores = jnp.dot(part, rows.T, preferred_element_type=jnp.float32) * scale
        top = lax.optimization_barrier(jnp.max(scores, axis=1))
        total = lax.optimization_barrier(jnp.sum(jnp.exp(scores - top[:, None]), axis=1))
        chosen = jnp.take_along_axis(scores, picks[:, None], axis=1)[:, 0]
        return (top, total, chosen)
    top, total, chosen = lax.map(block_scores, (particles.reshape(count // block, block, voxels), flat_ids.reshape(count // block, block)))
    top = top.reshape(count)
    total = total.reshape(count)
    chosen = chosen.reshape(count)
    gain = (weights * (classes * orients) * jnp.exp(chosen - top) / total).astype(jnp.bfloat16)
    member = class_ids[None, :] == jnp.arange(classes, dtype=jnp.int32)[:, None]
    summed = jnp.zeros((classes, voxels), jnp.float32)
    for step in range(-SHIFT, SHIFT + 1):
        coef = jnp.where(member & (offsets[None, :] == step), gain[None, :], jnp.zeros((), gain.dtype))
        moved = jnp.dot(coef, particles, preferred_element_type=jnp.float32)
        moved = jnp.roll(moved.reshape(classes, voxels // NX, NX), step, axis=2).reshape(classes, voxels)
        summed = summed + moved
    return summed / jnp.sqrt(jnp.float32(count / classes))
```

```python
import math

import jax
import jax.numpy as jnp
import numpy as np
from jax import lax
from jax.experimental import pallas as pl
from jax.experimental.pallas import tpu as pltpu
from jax.sharding import Mesh
from jax.sharding import PartitionSpec as P

NX = 64
SHIFT = 3
XH, YN, XL, ZN, CORES = 2, 4, 2, 8, 2
XN = XH * XL
ALL = ("xh", "y", "xl", "z", "core")
AX, AY, AZ = 0, 1, 2
SIZES = (XN, YN, ZN)
STAGES = ((AX, AY), (AY, AZ), (AZ, AX))


def flat_device(x, y, z, core):
    return (((x // XL * YN + y) * XL + x % XL) * ZN + z) * CORES + core


def pairs(move):
    out = []
    for x in range(XN):
        for y in range(YN):
            for z in range(ZN):
                for core in range(CORES):
                    (tx, ty, tz), tc = move([x, y, z], core)
                    out.append((flat_device(x, y, z, core), flat_device(tx % XN, ty % YN, tz % ZN, tc)))
    return out


def swap_cores(value):
    return lax.ppermute(value, ALL, pairs(lambda at, core: (at, 1 - core)))


class Piece:
    def __init__(self, rows, offsets):
        self.rows, self.offsets = rows, offsets

    def part(self, start, stop):
        return Piece(self.rows[start:stop], [o[start:stop] for o in self.offsets])

    def fetch(self, axes, steps):
        def move(at, core):
            at[axes[core]] -= steps
            return at, core

        moved = [o + steps * np.eye(4, dtype=np.int32)[axis] for o, axis in zip(self.offsets, axes)]
        return Piece(lax.ppermute(self.rows, ALL, pairs(move)), moved)


def join(pieces):
    return Piece(
        jnp.concatenate([p.rows for p in pieces], axis=0),
        [np.concatenate([p.offsets[c] for p in pieces], axis=0) for c in range(CORES)],
    )


def ring(piece, axes):
    half = piece.rows.shape[0] // 2
    ahead, behind = piece.fetch(axes, 1), piece.fetch(axes, -1)
    far_a = ahead.part(0, half).fetch(axes, 1)
    far_b = behind.part(half, 2 * half).fetch(axes, -1)
    return [piece, ahead, behind, far_a, far_b]


def row_ids(piece, here, local):
    core = here[3]
    d = jnp.where(core == 0, jnp.asarray(piece.offsets[0]), jnp.asarray(piece.offsets[1]))
    x, y, z = (here[0] + d[:, 0]) % XN, (here[1] + d[:, 1]) % YN, (here[2] + d[:, 2]) % ZN
    return flat_device(x, y, z, core) * local + d[:, 3]


def sums_kernel(key_ref, gain_ref, particles_ref, out_ref):
    steps = 2 * SHIFT + 1
    classes, width = out_ref.shape
    rows = lax.broadcasted_iota(jnp.int32, (steps * classes, key_ref.shape[1]), 0)
    coef = jnp.where(rows == key_ref[...], gain_ref[...], 0.0).astype(jnp.bfloat16)
    moved = jnp.dot(coef, particles_ref[...], preferred_element_type=jnp.float32)
    lane = lax.broadcasted_iota(jnp.int32, (classes, width), 1) % NX
    total = jnp.zeros((classes, width), jnp.float32)
    for k in range(steps):
        step = k - SHIFT
        part = moved[k * classes : (k + 1) * classes]
        if step == 0:
            total = total + part
            continue
        inside = (lane >= step) if step > 0 else (lane < NX + step)
        wrapped = step - NX if step > 0 else step + NX
        total = total + jnp.where(
            inside, pltpu.roll(part, step % width, 1), pltpu.roll(part, wrapped % width, 1)
        )
    out_ref[...] = total


def class_sums(key, gain, particles, classes):
    count, voxels = particles.shape
    width = 512
    return pl.pallas_call(
        sums_kernel,
        out_shape=jax.ShapeDtypeStruct((classes, voxels), jnp.float32),
        grid=(voxels // width,),
        in_specs=[
            pl.BlockSpec((1, count), lambda i: (0, 0)),
            pl.BlockSpec((1, count), lambda i: (0, 0)),
            pl.BlockSpec((count, width), lambda i: (0, i)),
        ],
        out_specs=pl.BlockSpec((classes, width), lambda i: (0, i)),
        name="class_sums",
    )(key, gain, particles)


def body(references, particles, class_ids, orient_ids, offsets, weights):
    per_owner, local, voxels = references.shape
    devices = XN * YN * ZN * CORES
    classes = per_owner * XH * YN
    orients = local * XL * ZN * CORES
    count = particles.shape[0]
    scale = 1.0 / math.sqrt(voxels)
    xh, y, xl, z, core = (lax.axis_index(a) for a in ALL)
    here = (xh * XL + xl, y, z, core)

    wanted = class_ids * orients + orient_ids
    other = swap_cores(particles)
    other_wanted = swap_cores(wanted.astype(jnp.float32)).astype(jnp.int32)

    start = np.zeros((local, 4), np.int32)
    start[:, 3] = np.arange(local)
    piece = Piece(references.reshape(local, voxels), [start, start])
    piece = join([piece, piece.fetch((AZ, AZ), ZN // 2)])
    first = STAGES[0]
    piece = join([piece, piece.fetch(first, 1), piece.fetch(first, -1), piece.fetch(first, 2)])
    piece = join(ring(piece, STAGES[1]))
    pieces = ring(piece, STAGES[2])

    def stats(part, ids, whose):
        scores = (
            lax.dot_general(
                part.rows, whose[0], (((1,), (1,)), ((), ())), preferred_element_type=jnp.float32
            )
            * scale
        )
        top = jnp.max(scores, axis=0)
        total = jnp.sum(jnp.exp(scores - top[None, :]), axis=0)
        chosen = jnp.sum(jnp.where(ids[:, None] == whose[1][None, :], scores, 0.0), axis=0)
        return top, total, chosen

    def merge(parts):
        tops = jnp.stack([p[0] for p in parts])
        totals = jnp.stack([p[1] for p in parts])
        chosen = jnp.stack([p[2] for p in parts])
        top = jnp.max(tops, axis=0)
        return top, jnp.sum(totals * jnp.exp(tops - top[None, :]), axis=0), jnp.sum(chosen, axis=0)

    mine, theirs = [], []
    for part in pieces:
        ids = row_ids(part, here, local)
        mine.append(stats(part, ids, (particles, wanted)))
        theirs.append(stats(part, ids, (other, other_wanted)))
    got = swap_cores(jnp.stack(merge(theirs)))
    top, total, chosen = merge([merge(mine), (got[0], got[1], got[2])])
    gain = (weights * (classes * orients) * jnp.exp(chosen - top) / total).astype(jnp.bfloat16)
    key = class_ids + classes * (offsets + SHIFT)
    partial_sums = class_sums(key[None, :], gain.astype(jnp.float32)[None, :], particles, classes)
    sent = partial_sums.reshape(devices, classes * voxels // devices)
    owned = jnp.sum(lax.all_to_all(sent, ALL, 0, 0, tiled=True), axis=0, keepdims=True)
    population = count * devices / classes
    return owned / jnp.sqrt(jnp.float32(population))


def solution(mesh):
    fine = Mesh(np.asarray(mesh.devices).reshape(XH, YN, XL, ZN, CORES), ALL)
    cls, ptl = ("xh", "y"), ("xl", "z", "core")
    placed = (P(cls, ptl, None), P(ALL, None), P(ALL), P(ALL), P(ALL), P(ALL))
    return jax.shard_map(
        body, mesh=fine, in_specs=placed, out_specs=P(cls, ptl), check_vma=False
    )
```

```python
import functools
import math

import jax
import jax.numpy as jnp
import numpy as np
from jax import lax
from jax.experimental import pallas as pl
from jax.experimental.pallas import tpu as pltpu
from jax.sharding import Mesh
from jax.sharding import PartitionSpec as P

NX = 64
SHIFT = 3
XH, YN, XL, ZN, CORES = 2, 4, 2, 8, 2
XN = XH * XL
ALL = ("xh", "y", "xl", "z", "core")
AX, AY, AZ = 0, 1, 2
SIZES = (XN, YN, ZN)
STAGES = ((AX, AY), (AY, AZ), (AZ, AX))


def flat_device(x, y, z, core):
    return (((x // XL * YN + y) * XL + x % XL) * ZN + z) * CORES + core


def pairs(move):
    out = []
    for x in range(XN):
        for y in range(YN):
            for z in range(ZN):
                for core in range(CORES):
                    (tx, ty, tz), tc = move([x, y, z], core)
                    out.append((flat_device(x, y, z, core), flat_device(tx % XN, ty % YN, tz % ZN, tc)))
    return out


def swap_cores(value):
    return lax.ppermute(value, ALL, pairs(lambda at, core: (at, 1 - core)))


class Piece:
    def __init__(self, rows, offsets):
        self.rows, self.offsets = rows, offsets

    def part(self, start, stop):
        return Piece(self.rows[start:stop], [o[start:stop] for o in self.offsets])

    def fetch(self, axes, steps):
        def move(at, core):
            at[axes[core]] -= steps
            return at, core

        moved = [o + steps * np.eye(4, dtype=np.int32)[axis] for o, axis in zip(self.offsets, axes)]
        return Piece(lax.ppermute(self.rows, ALL, pairs(move)), moved)


def join(pieces):
    return Piece(
        jnp.concatenate([p.rows for p in pieces], axis=0),
        [np.concatenate([p.offsets[c] for p in pieces], axis=0) for c in range(CORES)],
    )


def ring(piece, axes):
    half = piece.rows.shape[0] // 2
    ahead, behind = piece.fetch(axes, 1), piece.fetch(axes, -1)
    far_a = ahead.part(0, half).fetch(axes, 1)
    far_b = behind.part(half, 2 * half).fetch(axes, -1)
    return [piece, ahead, behind, far_a, far_b]


def row_ids(pieces, here, local):
    packed = []
    for core in range(CORES):
        d = np.concatenate([p.offsets[core] for p in pieces], axis=0)
        x, y, z = d[:, 0] % XN, d[:, 1] % YN, d[:, 2] % ZN
        packed.append((((x * YN + y) * ZN + z) * local + d[:, 3]).astype(np.int32))
    d = jnp.where(here[3] == 0, jnp.asarray(packed[0]), jnp.asarray(packed[1]))
    r, d = d % local, d // local
    z, d = (here[2] + d % ZN) % ZN, d // ZN
    y, x = (here[1] + d % YN) % YN, (here[0] + d // YN) % XN
    return (flat_device(x, y, z, here[3]) * local + r).astype(jnp.float32)[None, :]


LANES = 128
BLOCK = 256


def score_kernel(scale, n, first, ids_ref, wanted_ref, other_wanted_ref, own_ref, other_ref, *refs):
    pieces, refs = refs[:n], refs[n:]
    before, after = (None, None) if first else refs[:2], refs[-2:]
    count = own_ref.shape[0]
    ids, at = [], 0
    for piece in pieces:
        rows = piece.shape[0]
        column = jnp.broadcast_to(ids_ref[0:1, at : at + rows], (LANES, rows)).T
        ids.append(jnp.concatenate([column] * (BLOCK // LANES), axis=1))
        at += rows
    for side, (particles, wanted) in enumerate(((own_ref, wanted_ref), (other_ref, other_wanted_ref))):
        for start in range(0, count, BLOCK):
            cols = slice(start, start + BLOCK)
            block = particles[cols, :]
            want = wanted[0:1, cols]
            scores = [
                lax.dot_general(
                    piece[...], block, (((1,), (1,)), ((), ())), preferred_element_type=jnp.float32
                )
                * scale
                for piece in pieces
            ]
            top = functools.reduce(jnp.maximum, [jnp.max(s, axis=0, keepdims=True) for s in scores])
            if not first:
                old_top = before[side][0:1, cols]
                top = jnp.maximum(top, old_top)
            total = sum(jnp.sum(jnp.exp(s - top), axis=0, keepdims=True) for s in scores)
            chosen = sum(
                jnp.sum(jnp.where(i == want, s, 0.0), axis=0, keepdims=True) for i, s in zip(ids, scores)
            )
            if not first:
                total = total + before[side][1:2, cols] * jnp.exp(old_top - top)
                chosen = chosen + before[side][2:3, cols]
            after[side][0:1, cols] = top
            after[side][1:2, cols] = total
            after[side][2:3, cols] = chosen


def score(pieces, ids, wanted, other_wanted, own, other, before, scale):
    count, voxels = own.shape
    rows = sum(p.rows.shape[0] for p in pieces)
    whole = pl.BlockSpec(memory_space=pltpu.VMEM)
    operands = [ids, wanted, other_wanted, own, other, *(p.rows for p in pieces), *(before or ())]
    return pl.pallas_call(
        functools.partial(score_kernel, scale, len(pieces), before is None),
        out_shape=[jax.ShapeDtypeStruct((8, count), jnp.float32)] * 2,
        in_specs=[whole] * len(operands),
        out_specs=[whole] * 2,
        compiler_params=pltpu.CompilerParams(vmem_limit_bytes=28 << 20),
        cost_estimate=pl.CostEstimate(
            flops=4 * rows * count * voxels, transcendentals=2 * rows * count, bytes_accessed=rows * voxels * 2
        ),
        name="score",
    )(*operands)


def sums_kernel(classes, orients, key_ref, weights_ref, mine_ref, got_ref, particles_ref, out_ref):
    count, voxels = particles_ref.shape
    top = jnp.maximum(mine_ref[0:1, :], got_ref[0:1, :])
    total = mine_ref[1:2, :] * jnp.exp(mine_ref[0:1, :] - top) + got_ref[1:2, :] * jnp.exp(got_ref[0:1, :] - top)
    chosen = mine_ref[2:3, :] + got_ref[2:3, :]
    gain = weights_ref[...] * (classes * orients) * jnp.exp(chosen - top) / total
    steps = 2 * SHIFT + 1
    rows = lax.broadcasted_iota(jnp.int32, (steps * classes, count), 0)
    coef = jnp.where(rows == key_ref[...], gain, 0.0).astype(jnp.bfloat16)
    width = 512
    lane = lax.broadcasted_iota(jnp.int32, (classes, width), 1) % NX
    for base in range(0, voxels, width):
        moved = jnp.dot(coef, particles_ref[:, base : base + width], preferred_element_type=jnp.float32)
        summed = jnp.zeros((classes, width), jnp.float32)
        for k in range(steps):
            step = k - SHIFT
            part = moved[k * classes : (k + 1) * classes]
            if step != 0:
                inside = (lane >= step) if step > 0 else (lane < NX + step)
                wrapped = step - NX if step > 0 else step + NX
                part = jnp.where(
                    inside, pltpu.roll(part, step % width, 1), pltpu.roll(part, wrapped % width, 1)
                )
            summed = summed + part
        for j in range(width // LANES):
            out_ref[:, base // LANES + j, :] = summed[:, j * LANES : (j + 1) * LANES]


def class_sums(key, weights, mine, got, particles, classes, orients):
    count, voxels = particles.shape
    whole = pl.BlockSpec(memory_space=pltpu.VMEM)
    return pl.pallas_call(
        functools.partial(sums_kernel, classes, orients),
        out_shape=jax.ShapeDtypeStruct((classes, voxels // LANES, LANES), jnp.float32),
        in_specs=[whole] * 5,
        out_specs=whole,
        compiler_params=pltpu.CompilerParams(vmem_limit_bytes=16 << 20),
        name="class_sums",
    )(key, weights, mine, got, particles)


def body(references, particles, class_ids, orient_ids, offsets, weights):
    per_owner, local, voxels = references.shape
    devices = XN * YN * ZN * CORES
    classes = per_owner * XH * YN
    orients = local * XL * ZN * CORES
    count = particles.shape[0]
    scale = 1.0 / math.sqrt(voxels)
    xh, y, xl, z, core = (lax.axis_index(a) for a in ALL)
    here = (xh * XL + xl, y, z, core)

    other = swap_cores(particles)
    wanted = (class_ids * orients + orient_ids).astype(jnp.float32)[None, :]
    other_wanted = swap_cores(wanted)

    start = np.zeros((local, 4), np.int32)
    start[:, 3] = np.arange(local)
    piece = Piece(references.reshape(local, voxels), [start, start])
    piece = join([piece, piece.fetch((AZ, AZ), ZN // 2)])
    first = STAGES[0]
    piece = join([piece, piece.fetch(first, 1), piece.fetch(first, -1), piece.fetch(first, 2)])
    piece = join(ring(piece, STAGES[1]))
    pieces = ring(piece, STAGES[2])

    stats = None
    for group in (pieces[:1], pieces[1:3], pieces[3:]):
        ids = row_ids(group, here, local)
        stats = score(group, ids, wanted, other_wanted, particles, other, stats, scale)
    mine, theirs = stats
    got = swap_cores(theirs)
    key = class_ids + classes * (offsets + SHIFT)
    partial_sums = class_sums(key[None, :], weights[None, :], mine, got, particles, classes, orients)
    sent = partial_sums.reshape(devices, classes * voxels // devices)
    owned = jnp.sum(lax.all_to_all(sent, ALL, 0, 0, tiled=True), axis=0, keepdims=True)
    population = count * devices / classes
    return owned / jnp.sqrt(jnp.float32(population))


def solution(mesh):
    fine = Mesh(np.asarray(mesh.devices).reshape(XH, YN, XL, ZN, CORES), ALL)
    cls, ptl = ("xh", "y"), ("xl", "z", "core")
    placed = (P(cls, ptl, None), P(ALL, None), P(ALL), P(ALL), P(ALL), P(ALL))
    return jax.shard_map(
        body, mesh=fine, in_specs=placed, out_specs=P(cls, ptl), check_vma=False
    )
```

```python
import functools
import math

import jax
import jax.numpy as jnp
import numpy as np
from jax import lax
from jax.experimental import pallas as pl
from jax.experimental.pallas import tpu as pltpu
from jax.sharding import Mesh
from jax.sharding import PartitionSpec as P

NX = 64
SHIFT = 3
XH, YN, XL, ZN, CORES = 2, 4, 2, 8, 2
XN = XH * XL
ALL = ("xh", "y", "xl", "z", "core")
AX, AY, AZ = 0, 1, 2
SIZES = (XN, YN, ZN)
STAGES = ((AX, AY), (AY, AZ), (AZ, AX))


def flat_device(x, y, z, core):
    return (((x // XL * YN + y) * XL + x % XL) * ZN + z) * CORES + core


def pairs(move):
    out = []
    for x in range(XN):
        for y in range(YN):
            for z in range(ZN):
                for core in range(CORES):
                    (tx, ty, tz), tc = move([x, y, z], core)
                    out.append((flat_device(x, y, z, core), flat_device(tx % XN, ty % YN, tz % ZN, tc)))
    return out


def swap_cores(value):
    return lax.ppermute(value, ALL, pairs(lambda at, core: (at, 1 - core)))


class Piece:
    def __init__(self, rows, offsets):
        self.rows, self.offsets = rows, offsets

    def part(self, start, stop):
        return Piece(self.rows[start:stop], [o[start:stop] for o in self.offsets])

    def fetch(self, axes, steps):
        def move(at, core):
            at[axes[core]] -= steps
            return at, core

        moved = [o + steps * np.eye(4, dtype=np.int32)[axis] for o, axis in zip(self.offsets, axes)]
        return Piece(lax.ppermute(self.rows, ALL, pairs(move)), moved)


def join(pieces):
    return Piece(
        jnp.concatenate([p.rows for p in pieces], axis=0),
        [np.concatenate([p.offsets[c] for p in pieces], axis=0) for c in range(CORES)],
    )


def ring(piece, axes):
    half = piece.rows.shape[0] // 2
    ahead, behind = piece.fetch(axes, 1), piece.fetch(axes, -1)
    far_a = ahead.part(0, half).fetch(axes, 1)
    far_b = behind.part(half, 2 * half).fetch(axes, -1)
    return [piece, ahead, behind, far_a, far_b]


def row_ids(pieces, here, local):
    packed = []
    for core in range(CORES):
        d = np.concatenate([p.offsets[core] for p in pieces], axis=0)
        x, y, z = d[:, 0] % XN, d[:, 1] % YN, d[:, 2] % ZN
        packed.append((((x * YN + y) * ZN + z) * local + d[:, 3]).astype(np.int32))
    d = jnp.where(here[3] == 0, jnp.asarray(packed[0]), jnp.asarray(packed[1]))
    r, d = d % local, d // local
    z, d = (here[2] + d % ZN) % ZN, d // ZN
    y, x = (here[1] + d % YN) % YN, (here[0] + d // YN) % XN
    return (flat_device(x, y, z, here[3]) * local + r).astype(jnp.float32)[None, :]


LANES = 128
BLOCK = 256


def score_kernel(scale, n, first, ids_ref, wanted_ref, other_wanted_ref, own_ref, other_ref, *refs):
    pieces, refs = refs[:n], refs[n:]
    before, after = (None, None) if first else refs[:2], refs[-2:]
    count = own_ref.shape[0]
    rows = sum(piece.shape[0] for piece in pieces)
    column = jnp.broadcast_to(ids_ref[...], (LANES, rows)).T
    ids = jnp.concatenate([column] * (BLOCK // LANES), axis=1)
    held = jnp.concatenate([piece[...] for piece in pieces], axis=0)
    for side, (particles, wanted) in enumerate(((own_ref, wanted_ref), (other_ref, other_wanted_ref))):
        for start in range(0, count, BLOCK):
            cols = slice(start, start + BLOCK)
            block = particles[cols, :]
            want = wanted[0:1, cols]
            scores = scale * lax.dot_general(
                held, block, (((1,), (1,)), ((), ())), preferred_element_type=jnp.float32
            )
            top = jnp.max(scores, axis=0, keepdims=True)
            if not first:
                old_top = before[side][0:1, cols]
                top = jnp.maximum(top, old_top)
            total = jnp.sum(jnp.exp(scores - top), axis=0, keepdims=True)
            chosen = jnp.sum(jnp.where(ids == want, scores, 0.0), axis=0, keepdims=True)
            if not first:
                total = total + before[side][1:2, cols] * jnp.exp(old_top - top)
                chosen = chosen + before[side][2:3, cols]
            after[side][0:1, cols] = top
            after[side][1:2, cols] = total
            after[side][2:3, cols] = chosen


def score(pieces, ids, wanted, other_wanted, own, other, before, scale):
    count, voxels = own.shape
    rows = sum(p.rows.shape[0] for p in pieces)
    whole = pl.BlockSpec(memory_space=pltpu.VMEM)
    operands = [ids, wanted, other_wanted, own, other, *(p.rows for p in pieces), *(before or ())]
    return pl.pallas_call(
        functools.partial(score_kernel, scale, len(pieces), before is None),
        out_shape=[jax.ShapeDtypeStruct((8, count), jnp.float32)] * 2,
        in_specs=[whole] * len(operands),
        out_specs=[whole] * 2,
        compiler_params=pltpu.CompilerParams(vmem_limit_bytes=16 << 20),
        cost_estimate=pl.CostEstimate(
            flops=4 * rows * count * voxels, transcendentals=2 * rows * count, bytes_accessed=rows * voxels * 2
        ),
        name="score",
    )(*operands)


def sums_kernel(classes, orients, key_ref, weights_ref, mine_ref, got_ref, particles_ref, out_ref):
    count, voxels = particles_ref.shape
    top = jnp.maximum(mine_ref[0:1, :], got_ref[0:1, :])
    total = mine_ref[1:2, :] * jnp.exp(mine_ref[0:1, :] - top) + got_ref[1:2, :] * jnp.exp(got_ref[0:1, :] - top)
    chosen = mine_ref[2:3, :] + got_ref[2:3, :]
    gain = weights_ref[...] * (classes * orients) * jnp.exp(chosen - top) / total
    steps = 2 * SHIFT + 1
    rows = lax.broadcasted_iota(jnp.int32, (steps * classes, count), 0)
    coef = jnp.where(rows == key_ref[...], gain, 0.0).astype(jnp.bfloat16)
    width = 512
    lane = lax.broadcasted_iota(jnp.int32, (classes, width), 1) % NX
    for base in range(0, voxels, width):
        moved = jnp.dot(coef, particles_ref[:, base : base + width], preferred_element_type=jnp.float32)
        summed = jnp.zeros((classes, width), jnp.float32)
        for k in range(steps):
            step = k - SHIFT
            part = moved[k * classes : (k + 1) * classes]
            if step != 0:
                inside = (lane >= step) if step > 0 else (lane < NX + step)
                wrapped = step - NX if step > 0 else step + NX
                part = jnp.where(
                    inside, pltpu.roll(part, step % width, 1), pltpu.roll(part, wrapped % width, 1)
                )
            summed = summed + part
        for j in range(width // LANES):
            out_ref[:, base // LANES + j, :] = summed[:, j * LANES : (j + 1) * LANES]


def class_sums(key, weights, mine, got, particles, classes, orients):
    count, voxels = particles.shape
    whole = pl.BlockSpec(memory_space=pltpu.VMEM)
    return pl.pallas_call(
        functools.partial(sums_kernel, classes, orients),
        out_shape=jax.ShapeDtypeStruct((classes, voxels // LANES, LANES), jnp.float32),
        in_specs=[whole] * 5,
        out_specs=whole,
        compiler_params=pltpu.CompilerParams(vmem_limit_bytes=16 << 20),
        name="class_sums",
    )(key, weights, mine, got, particles)


def body(references, particles, class_ids, orient_ids, offsets, weights):
    per_owner, local, voxels = references.shape
    devices = XN * YN * ZN * CORES
    classes = per_owner * XH * YN
    orients = local * XL * ZN * CORES
    count = particles.shape[0]
    scale = 1.0 / math.sqrt(voxels)
    xh, y, xl, z, core = (lax.axis_index(a) for a in ALL)
    here = (xh * XL + xl, y, z, core)

    other = swap_cores(particles)
    wanted = (class_ids * orients + orient_ids).astype(jnp.float32)[None, :]
    other_wanted = swap_cores(wanted)

    start = np.zeros((local, 4), np.int32)
    start[:, 3] = np.arange(local)
    piece = Piece(references.reshape(local, voxels), [start, start])
    piece = join([piece, piece.fetch((AZ, AZ), ZN // 2)])
    first = STAGES[0]
    piece = join([piece, piece.fetch(first, 1), piece.fetch(first, -1), piece.fetch(first, 2)])
    near, ahead, behind, far_a, far_b = ring(piece, STAGES[1])
    last = STAGES[2]
    one, two = join([near, ahead]), join([behind, far_a, far_b])
    ahead_one, behind_one = one.fetch(last, 1), one.fetch(last, -1)
    ahead_two, behind_two = two.fetch(last, 1), two.fetch(last, -1)
    far_one, far_two = ahead_one.fetch(last, 1), behind_two.fetch(last, -1)

    stats = None
    for group in ((one, two), (ahead_one, behind_one), (ahead_two, behind_two), (far_one, far_two)):
        ids = row_ids(group, here, local)
        stats = score(group, ids, wanted, other_wanted, particles, other, stats, scale)
    mine, theirs = stats
    got = swap_cores(theirs)
    key = class_ids + classes * (offsets + SHIFT)
    partial_sums = class_sums(key[None, :], weights[None, :], mine, got, particles, classes, orients)
    sent = partial_sums.reshape(devices, classes * voxels // devices)
    owned = jnp.sum(lax.all_to_all(sent, ALL, 0, 0, tiled=True), axis=0, keepdims=True)
    population = count * devices / classes
    return owned / jnp.sqrt(jnp.float32(population))


def solution(mesh):
    fine = Mesh(np.asarray(mesh.devices).reshape(XH, YN, XL, ZN, CORES), ALL)
    cls, ptl = ("xh", "y"), ("xl", "z", "core")
    placed = (P(cls, ptl, None), P(ALL, None), P(ALL), P(ALL), P(ALL), P(ALL))
    return jax.shard_map(
        body, mesh=fine, in_specs=placed, out_specs=P(cls, ptl), check_vma=False
    )
```

```python
import functools
import math

import jax
import jax.numpy as jnp
import numpy as np
from jax import lax
from jax.experimental import pallas as pl
from jax.experimental.pallas import tpu as pltpu
from jax.sharding import Mesh
from jax.sharding import PartitionSpec as P

NX = 64
SHIFT = 3
XH, YN, XL, ZN, CORES = 2, 4, 2, 8, 2
XN = XH * XL
ALL = ("xh", "y", "xl", "z", "core")
AX, AY, AZ = 0, 1, 2
SIZES = (XN, YN, ZN)
STAGES = ((AX, AY), (AY, AZ), (AZ, AX))


def flat_device(x, y, z, core):
    return (((x // XL * YN + y) * XL + x % XL) * ZN + z) * CORES + core


def pairs(move):
    out = []
    for x in range(XN):
        for y in range(YN):
            for z in range(ZN):
                for core in range(CORES):
                    (tx, ty, tz), tc = move([x, y, z], core)
                    out.append((flat_device(x, y, z, core), flat_device(tx % XN, ty % YN, tz % ZN, tc)))
    return out


def swap_cores(value):
    return lax.ppermute(value, ALL, pairs(lambda at, core: (at, 1 - core)))


class Piece:
    def __init__(self, rows, offsets):
        self.rows, self.offsets = rows, offsets

    def part(self, start, stop):
        return Piece(self.rows[start:stop], [o[start:stop] for o in self.offsets])

    def fetch(self, axes, steps):
        def move(at, core):
            at[axes[core]] -= steps
            return at, core

        moved = [o + steps * np.eye(4, dtype=np.int32)[axis] for o, axis in zip(self.offsets, axes)]
        return Piece(lax.ppermute(self.rows, ALL, pairs(move)), moved)


def join(pieces):
    return Piece(
        jnp.concatenate([p.rows for p in pieces], axis=0),
        [np.concatenate([p.offsets[c] for p in pieces], axis=0) for c in range(CORES)],
    )


def row_ids(pieces, here, local):
    packed = []
    for core in range(CORES):
        d = np.concatenate([p.offsets[core] for p in pieces], axis=0)
        x, y, z = d[:, 0] % XN, d[:, 1] % YN, d[:, 2] % ZN
        packed.append((((x * YN + y) * ZN + z) * local + d[:, 3]).astype(np.int32))
    d = jnp.where(here[3] == 0, jnp.asarray(packed[0]), jnp.asarray(packed[1]))
    r, d = d % local, d // local
    z, d = (here[2] + d % ZN) % ZN, d // ZN
    y, x = (here[1] + d % YN) % YN, (here[0] + d // YN) % XN
    return (flat_device(x, y, z, here[3]) * local + r).astype(jnp.float32)[None, :]


LANES = 128
BLOCK = 256


def score_kernel(scale, n, first, ids_ref, wanted_ref, other_wanted_ref, own_ref, other_ref, *refs):
    pieces, refs = refs[:n], refs[n:]
    if first:
        before, (mine, theirs, kept, arrived) = None, refs
        copy = pltpu.make_async_copy(other_ref, kept, arrived)
        copy.start()
    else:
        before, (mine, theirs), kept = refs[:2], refs[2:], other_ref
    count = own_ref.shape[0]
    rows = sum(piece.shape[0] for piece in pieces)
    column = jnp.broadcast_to(ids_ref[...], (LANES, rows)).T
    ids = jnp.concatenate([column] * (BLOCK // LANES), axis=1)
    held = jnp.concatenate([piece[...] for piece in pieces], axis=0)
    for side, (particles, wanted, after) in enumerate(
        ((own_ref, wanted_ref, mine), (kept, other_wanted_ref, theirs))
    ):
        if first and side == 1:
            copy.wait()
        for start in range(0, count, BLOCK):
            cols = slice(start, start + BLOCK)
            block = particles[cols, :]
            want = wanted[0:1, cols]
            scores = scale * lax.dot_general(
                held, block, (((1,), (1,)), ((), ())), preferred_element_type=jnp.float32
            )
            top = jnp.max(scores, axis=0, keepdims=True)
            if not first:
                old_top = before[side][0:1, cols]
                top = jnp.maximum(top, old_top)
            total = jnp.sum(jnp.exp(scores - top), axis=0, keepdims=True)
            chosen = jnp.sum(jnp.where(ids == want, scores, 0.0), axis=0, keepdims=True)
            if not first:
                total = total + before[side][1:2, cols] * jnp.exp(old_top - top)
                chosen = chosen + before[side][2:3, cols]
            after[0:1, cols] = top
            after[1:2, cols] = total
            after[2:3, cols] = chosen


def score(pieces, ids, wanted, other_wanted, own, other, before, scale):
    count, voxels = own.shape
    rows = sum(p.rows.shape[0] for p in pieces)
    first = before is None
    whole = pl.BlockSpec(memory_space=pltpu.VMEM)
    operands = [ids, wanted, other_wanted, own, other, *(p.rows for p in pieces), *(before or ())]
    in_specs = [whole] * len(operands)
    out_shape = [jax.ShapeDtypeStruct((8, count), jnp.float32)] * 2
    if first:
        in_specs[4] = pl.BlockSpec(memory_space=pl.ANY)
        out_shape.append(jax.ShapeDtypeStruct(other.shape, other.dtype))
    return pl.pallas_call(
        functools.partial(score_kernel, scale, len(pieces), first),
        out_shape=out_shape,
        in_specs=in_specs,
        out_specs=[whole] * len(out_shape),
        scratch_shapes=[pltpu.SemaphoreType.DMA] if first else [],
        compiler_params=pltpu.CompilerParams(vmem_limit_bytes=16 << 20),
        cost_estimate=pl.CostEstimate(
            flops=4 * rows * count * voxels, transcendentals=2 * rows * count, bytes_accessed=rows * voxels * 2
        ),
        name="score",
    )(*operands)


def sums_kernel(classes, orients, key_ref, weights_ref, mine_ref, got_ref, particles_ref, out_ref):
    count, voxels = particles_ref.shape
    top = jnp.maximum(mine_ref[0:1, :], got_ref[0:1, :])
    total = mine_ref[1:2, :] * jnp.exp(mine_ref[0:1, :] - top) + got_ref[1:2, :] * jnp.exp(got_ref[0:1, :] - top)
    chosen = mine_ref[2:3, :] + got_ref[2:3, :]
    gain = weights_ref[...] * (classes * orients) * jnp.exp(chosen - top) / total
    steps = 2 * SHIFT + 1
    rows = lax.broadcasted_iota(jnp.int32, (steps * classes, count), 0)
    coef = jnp.where(rows == key_ref[...], gain, 0.0).astype(jnp.bfloat16)
    width = 512
    lane = lax.broadcasted_iota(jnp.int32, (classes, width), 1) % NX
    for base in range(0, voxels, width):
        moved = jnp.dot(coef, particles_ref[:, base : base + width], preferred_element_type=jnp.float32)
        summed = jnp.zeros((classes, width), jnp.float32)
        for k in range(steps):
            step = k - SHIFT
            part = moved[k * classes : (k + 1) * classes]
            if step != 0:
                inside = (lane >= step) if step > 0 else (lane < NX + step)
                wrapped = step - NX if step > 0 else step + NX
                part = jnp.where(
                    inside, pltpu.roll(part, step % width, 1), pltpu.roll(part, wrapped % width, 1)
                )
            summed = summed + part
        for j in range(width // LANES):
            out_ref[:, base // LANES + j, :] = summed[:, j * LANES : (j + 1) * LANES]


def class_sums(key, weights, mine, got, particles, classes, orients):
    count, voxels = particles.shape
    whole = pl.BlockSpec(memory_space=pltpu.VMEM)
    return pl.pallas_call(
        functools.partial(sums_kernel, classes, orients),
        out_shape=jax.ShapeDtypeStruct((classes, voxels // LANES, LANES), jnp.float32),
        in_specs=[whole] * 5,
        out_specs=whole,
        compiler_params=pltpu.CompilerParams(vmem_limit_bytes=16 << 20),
        name="class_sums",
    )(key, weights, mine, got, particles)


def body(references, particles, class_ids, orient_ids, offsets, weights):
    per_owner, local, voxels = references.shape
    devices = XN * YN * ZN * CORES
    classes = per_owner * XH * YN
    orients = local * XL * ZN * CORES
    count = particles.shape[0]
    scale = 1.0 / math.sqrt(voxels)
    xh, y, xl, z, core = (lax.axis_index(a) for a in ALL)
    here = (xh * XL + xl, y, z, core)

    other = swap_cores(particles)
    wanted = (class_ids * orients + orient_ids).astype(jnp.float32)[None, :]
    other_wanted = swap_cores(wanted)

    start = np.zeros((local, 4), np.int32)
    start[:, 3] = np.arange(local)
    piece = Piece(references.reshape(local, voxels), [start, start])
    piece = join([piece, piece.fetch((AZ, AZ), ZN // 2)])
    first = STAGES[0]
    piece = join([piece, piece.fetch(first, 1), piece.fetch(first, -1), piece.fetch(first, 2)])

    def take(group, kept, stats):
        ids = row_ids(group, here, local)
        out = score(group, ids, wanted, other_wanted, particles, kept, stats, scale)
        return (out[2] if stats is None else kept), out[:2]

    near, half = piece, piece.rows.shape[0] // 2
    ahead, behind = near.fetch(STAGES[1], 1), near.fetch(STAGES[1], -1)
    kept, stats = take([near], other, None)
    ahead.rows, behind.rows, stats = lax.optimization_barrier((ahead.rows, behind.rows, stats))
    far_a = ahead.part(0, half).fetch(STAGES[1], 1)
    far_b = behind.part(half, 2 * half).fetch(STAGES[1], -1)
    last = STAGES[2]
    chunks = [near, join([ahead, behind]), join([far_a, far_b])]
    next_, prev = [c.fetch(last, 1) for c in chunks], [c.fetch(last, -1) for c in chunks]
    far = [prev[0].fetch(last, -1), next_[1].fetch(last, 1), prev[2].fetch(last, -1)]
    for group in (
        chunks[1:] + [next_[0], prev[0]],
        [next_[1], prev[1]],
        [next_[2], prev[2], far[0]],
        far[1:],
    ):
        kept, stats = take(group, kept, stats)
    mine, theirs = stats
    got = swap_cores(theirs)
    key = class_ids + classes * (offsets + SHIFT)
    partial_sums = class_sums(key[None, :], weights[None, :], mine, got, particles, classes, orients)
    sent = partial_sums.reshape(devices, classes * voxels // devices)
    owned = jnp.sum(lax.all_to_all(sent, ALL, 0, 0, tiled=True), axis=0, keepdims=True)
    population = count * devices / classes
    return owned / jnp.sqrt(jnp.float32(population))


def solution(mesh):
    fine = Mesh(np.asarray(mesh.devices).reshape(XH, YN, XL, ZN, CORES), ALL)
    cls, ptl = ("xh", "y"), ("xl", "z", "core")
    placed = (P(cls, ptl, None), P(ALL, None), P(ALL), P(ALL), P(ALL), P(ALL))
    return jax.shard_map(
        body, mesh=fine, in_specs=placed, out_specs=P(cls, ptl), check_vma=False
    )
```

```python
import functools
import math

import jax
import jax.numpy as jnp
import numpy as np
from jax import lax
from jax.experimental import pallas as pl
from jax.experimental.pallas import tpu as pltpu
from jax.sharding import Mesh
from jax.sharding import PartitionSpec as P

NX = 64
SHIFT = 3
XH, YN, XL, ZN, CORES = 2, 4, 2, 8, 2
XN = XH * XL
ALL = ("xh", "y", "xl", "z", "core")
AX, AY, AZ = 0, 1, 2
SIZES = (XN, YN, ZN)
STAGES = ((AX, AZ), (AY, AY), (AZ, AX))


def flat_device(x, y, z, core):
    return (((x // XL * YN + y) * XL + x % XL) * ZN + z) * CORES + core


def pairs(move):
    out = []
    for x in range(XN):
        for y in range(YN):
            for z in range(ZN):
                for core in range(CORES):
                    (tx, ty, tz), tc = move([x, y, z], core)
                    out.append((flat_device(x, y, z, core), flat_device(tx % XN, ty % YN, tz % ZN, tc)))
    return out


def swap_cores(value):
    return lax.ppermute(value, ALL, pairs(lambda at, core: (at, 1 - core)))


class Piece:
    def __init__(self, rows, offsets):
        self.rows, self.offsets = rows, offsets

    def part(self, start, stop):
        rows = None if self.rows is None else self.rows[start:stop]
        return Piece(rows, [o[start:stop] for o in self.offsets])

    def fetch(self, axes, steps):
        def move(at, core):
            at[axes[core]] -= steps
            return at, core

        moved = [o + steps * np.eye(4, dtype=np.int32)[axis] for o, axis in zip(self.offsets, axes)]
        rows = None if self.rows is None else lax.ppermute(self.rows, ALL, pairs(move))
        return Piece(rows, moved)


def join(pieces):
    rows = None if pieces[0].rows is None else jnp.concatenate([p.rows for p in pieces], axis=0)
    offsets = [np.concatenate([p.offsets[c] for p in pieces], axis=0) for c in range(CORES)]
    return Piece(rows, offsets)


def together(pieces):
    if pieces[0].rows is not None:
        for piece, rows in zip(pieces, lax.optimization_barrier([p.rows for p in pieces])):
            piece.rows = rows


def spread(piece):
    piece = join([piece, piece.fetch((AZ, AZ), ZN // 2)])
    return [piece] + [piece.fetch(STAGES[0], steps) for steps in (1, -1, 2)]


def gather(near, first):
    near, half = join(near), sum(len(p.offsets[0]) for p in near) // 2
    last = STAGES[2]
    ahead, behind = near.fetch(STAGES[1], 1), near.fetch(STAGES[1], -1)
    next_, prev = [near.fetch(last, 1)], [near.fetch(last, -1)]
    together([ahead, behind, next_[0], prev[0]])
    far_a = ahead.part(0, half).fetch(STAGES[1], 1)
    far_b = behind.part(half, 2 * half).fetch(STAGES[1], -1)
    one = join([ahead, behind])
    far_a, far_b = first([near, one], far_a, far_b)
    chunks = [near, one, join([far_a, far_b])]
    for chunk in chunks[1:]:
        next_.append(chunk.fetch(last, 1))
        prev.append(chunk.fetch(last, -1))
    if near.rows is not None:
        next_[1].rows, _ = lax.optimization_barrier((next_[1].rows, chunks[2].rows))
        prev[0].rows, _ = lax.optimization_barrier((prev[0].rows, chunks[2].rows))
    far = [prev[0].fetch(last, -1), next_[1].fetch(last, 1), prev[2].fetch(last, -1)]
    return (
        chunks[:2],
        [chunks[2], next_[0], prev[0], next_[1], prev[1]],
        [next_[2], prev[2], *far],
    )


def row_ids(groups, here, local):
    packed = []
    for core in range(CORES):
        parts = []
        for group in groups:
            d = np.concatenate([p.offsets[core] for p in group], axis=0)
            x, y, z = d[:, 0] % XN, d[:, 1] % YN, d[:, 2] % ZN
            rel = (((x * YN + y) * ZN + z) * local + d[:, 3]).astype(np.int32)
            parts.append(np.pad(rel, (0, -len(rel) % LANES)))
        packed.append(np.concatenate(parts))
    d = jnp.where(here[3] == 0, jnp.asarray(packed[0]), jnp.asarray(packed[1]))
    r, d = d % local, d // local
    z, d = (here[2] + d % ZN) % ZN, d // ZN
    y, x = (here[1] + d % YN) % YN, (here[0] + d // YN) % XN
    return (flat_device(x, y, z, here[3]) * local + r).astype(jnp.float32)[None, :]


LANES = 128
BLOCK = 256


def score_kernel(scale, n, first, at, ids_ref, wanted_ref, other_wanted_ref, own_ref, other_ref, *refs):
    pieces, refs = refs[:n], refs[n:]
    if first:
        before, (mine, theirs, kept, arrived) = None, refs
        copy = pltpu.make_async_copy(other_ref, kept, arrived)
        copy.start()
    else:
        before, (mine, theirs), kept = refs[:2], refs[2:], other_ref
    count = own_ref.shape[0]
    rows = sum(piece.shape[0] for piece in pieces)
    whole = -(-rows // LANES) * LANES
    column = jnp.broadcast_to(ids_ref[0:1, at : at + whole], (LANES, whole)).T[:rows]
    ids = jnp.concatenate([column] * (BLOCK // LANES), axis=1)
    held = jnp.concatenate([piece[...] for piece in pieces], axis=0)
    for side, (particles, wanted, after) in enumerate(
        ((own_ref, wanted_ref, mine), (kept, other_wanted_ref, theirs))
    ):
        if first and side == 1:
            copy.wait()
        for start in range(0, count, BLOCK):
            cols = slice(start, start + BLOCK)
            block = particles[cols, :]
            want = wanted[0:1, cols]
            scores = scale * lax.dot_general(
                held, block, (((1,), (1,)), ((), ())), preferred_element_type=jnp.float32
            )
            top = jnp.max(scores, axis=0, keepdims=True)
            if not first:
                old_top = before[side][0:1, cols]
                top = jnp.maximum(top, old_top)
            total = jnp.sum(jnp.exp(scores - top), axis=0, keepdims=True)
            chosen = jnp.sum(jnp.where(ids == want, scores, 0.0), axis=0, keepdims=True)
            if not first:
                total = total + before[side][1:2, cols] * jnp.exp(old_top - top)
                chosen = chosen + before[side][2:3, cols]
            after[0:1, cols] = top
            after[1:2, cols] = total
            after[2:3, cols] = chosen


def score(pieces, ids, at, wanted, other_wanted, own, other, before, scale):
    count, voxels = own.shape
    rows = sum(p.rows.shape[0] for p in pieces)
    first = before is None
    whole = pl.BlockSpec(memory_space=pltpu.VMEM)
    operands = [ids, wanted, other_wanted, own, other, *(p.rows for p in pieces), *(before or ())]
    in_specs = [whole] * len(operands)
    out_shape = [jax.ShapeDtypeStruct((8, count), jnp.float32)] * 2
    if first:
        in_specs[4] = pl.BlockSpec(memory_space=pl.ANY)
        out_shape.append(jax.ShapeDtypeStruct(other.shape, other.dtype))
    return pl.pallas_call(
        functools.partial(score_kernel, scale, len(pieces), first, at),
        out_shape=out_shape,
        in_specs=in_specs,
        out_specs=[whole] * len(out_shape),
        scratch_shapes=[pltpu.SemaphoreType.DMA] if first else [],
        compiler_params=pltpu.CompilerParams(vmem_limit_bytes=16 << 20),
        cost_estimate=pl.CostEstimate(
            flops=4 * rows * count * voxels, transcendentals=2 * rows * count, bytes_accessed=rows * voxels * 2
        ),
        name="score",
    )(*operands)


def sums_kernel(classes, orients, key_ref, weights_ref, mine_ref, got_ref, particles_ref, out_ref):
    count, voxels = particles_ref.shape
    top = jnp.maximum(mine_ref[0:1, :], got_ref[0:1, :])
    total = mine_ref[1:2, :] * jnp.exp(mine_ref[0:1, :] - top) + got_ref[1:2, :] * jnp.exp(got_ref[0:1, :] - top)
    chosen = mine_ref[2:3, :] + got_ref[2:3, :]
    gain = weights_ref[...] * (classes * orients) * jnp.exp(chosen - top) / total
    steps = 2 * SHIFT + 1
    rows = lax.broadcasted_iota(jnp.int32, (steps * classes, count), 0)
    coef = jnp.where(rows == key_ref[...], gain, 0.0).astype(jnp.bfloat16)
    width = 512
    lane = lax.broadcasted_iota(jnp.int32, (classes, width), 1) % NX
    for base in range(0, voxels, width):
        moved = jnp.dot(coef, particles_ref[:, base : base + width], preferred_element_type=jnp.float32)
        summed = jnp.zeros((classes, width), jnp.float32)
        for k in range(steps):
            step = k - SHIFT
            part = moved[k * classes : (k + 1) * classes]
            if step != 0:
                inside = (lane >= step) if step > 0 else (lane < NX + step)
                wrapped = step - NX if step > 0 else step + NX
                part = jnp.where(
                    inside, pltpu.roll(part, step % width, 1), pltpu.roll(part, wrapped % width, 1)
                )
            summed = summed + part
        for j in range(width // LANES):
            out_ref[:, base // LANES + j, :] = summed[:, j * LANES : (j + 1) * LANES]


def class_sums(key, weights, mine, got, particles, classes, orients):
    count, voxels = particles.shape
    whole = pl.BlockSpec(memory_space=pltpu.VMEM)
    return pl.pallas_call(
        functools.partial(sums_kernel, classes, orients),
        out_shape=jax.ShapeDtypeStruct((classes, voxels // LANES, LANES), jnp.float32),
        in_specs=[whole] * 5,
        out_specs=whole,
        compiler_params=pltpu.CompilerParams(vmem_limit_bytes=16 << 20),
        name="class_sums",
    )(key, weights, mine, got, particles)


def body(references, particles, class_ids, orient_ids, offsets, weights):
    per_owner, local, voxels = references.shape
    devices = XN * YN * ZN * CORES
    classes = per_owner * XH * YN
    orients = local * XL * ZN * CORES
    count = particles.shape[0]
    scale = 1.0 / math.sqrt(voxels)
    xh, y, xl, z, core = (lax.axis_index(a) for a in ALL)
    here = (xh * XL + xl, y, z, core)

    other = swap_cores(particles)
    wanted = (class_ids * orients + orient_ids).astype(jnp.float32)[None, :]
    key = (class_ids + classes * (offsets + SHIFT))[None, :]
    other_wanted = swap_cores(wanted)

    start = np.zeros((local, 4), np.int32)
    start[:, 3] = np.arange(local)
    dry = gather(spread(Piece(None, [start, start])), lambda group, *halves: halves)
    ids = row_ids(dry, here, local)
    near = spread(Piece(references.reshape(local, voxels), [start, start]))
    rows, ids, wanted, key = lax.optimization_barrier((near[-1].rows, ids, wanted, key))
    near[-1].rows = rows
    kept, stats, at = other, None, 0

    def take(group):
        nonlocal kept, stats, at
        out = score(group, ids, at, wanted, other_wanted, particles, kept, stats, scale)
        kept, stats = (out[2] if stats is None else kept), out[:2]
        count_rows = sum(len(p.offsets[0]) for p in group)
        at += -(-count_rows // LANES) * LANES

    def first(group, far_a, far_b):
        nonlocal stats
        take(group)
        far_a.rows, far_b.rows, stats = lax.optimization_barrier((far_a.rows, far_b.rows, stats))
        return far_a, far_b

    for group in gather(near, first)[1:]:
        take(group)
    mine, theirs = stats
    got = swap_cores(theirs)
    partial_sums = class_sums(key, weights[None, :], mine, got, particles, classes, orients)
    sent = partial_sums.reshape(devices, classes * voxels // devices)
    owned = jnp.sum(lax.all_to_all(sent, ALL, 0, 0, tiled=True), axis=0, keepdims=True)
    population = count * devices / classes
    return owned / jnp.sqrt(jnp.float32(population))


def solution(mesh):
    fine = Mesh(np.asarray(mesh.devices).reshape(XH, YN, XL, ZN, CORES), ALL)
    cls, ptl = ("xh", "y"), ("xl", "z", "core")
    placed = (P(cls, ptl, None), P(ALL, None), P(ALL), P(ALL), P(ALL), P(ALL))
    return jax.shard_map(
        body, mesh=fine, in_specs=placed, out_specs=P(cls, ptl), check_vma=False
    )
```

```python
import functools
import math

import jax
import jax.numpy as jnp
import numpy as np
from jax import lax
from jax.experimental import pallas as pl
from jax.experimental.pallas import tpu as pltpu
from jax.sharding import Mesh
from jax.sharding import PartitionSpec as P

NX = 64
SHIFT = 3
XH, YN, XL, ZN, CORES = 2, 4, 2, 8, 2
XN = XH * XL
ALL = ("xh", "y", "xl", "z", "core")
AX, AY, AZ = 0, 1, 2
SIZES = (XN, YN, ZN)
STAGES = ((AX, AZ), (AY, AY), (AZ, AX))


def flat_device(x, y, z, core):
    return (((x // XL * YN + y) * XL + x % XL) * ZN + z) * CORES + core


def pairs(move):
    out = []
    for x in range(XN):
        for y in range(YN):
            for z in range(ZN):
                for core in range(CORES):
                    (tx, ty, tz), tc = move([x, y, z], core)
                    out.append((flat_device(x, y, z, core), flat_device(tx % XN, ty % YN, tz % ZN, tc)))
    return out


def swap_cores(value):
    return lax.ppermute(value, ALL, pairs(lambda at, core: (at, 1 - core)))


class Piece:
    def __init__(self, rows, offsets):
        self.rows, self.offsets = rows, offsets

    def part(self, start, stop):
        rows = None if self.rows is None else self.rows[start:stop]
        return Piece(rows, [o[start:stop] for o in self.offsets])

    def fetch(self, axes, steps):
        def move(at, core):
            at[axes[core]] -= steps
            return at, core

        moved = [o + steps * np.eye(4, dtype=np.int32)[axis] for o, axis in zip(self.offsets, axes)]
        rows = None if self.rows is None else lax.ppermute(self.rows, ALL, pairs(move))
        return Piece(rows, moved)


def join(pieces):
    rows = None if pieces[0].rows is None else jnp.concatenate([p.rows for p in pieces], axis=0)
    offsets = [np.concatenate([p.offsets[c] for p in pieces], axis=0) for c in range(CORES)]
    return Piece(rows, offsets)


def spread(piece):
    piece = join([piece, piece.fetch((AZ, AZ), ZN // 2)])
    return [piece] + [piece.fetch(STAGES[0], steps) for steps in (1, -1, 2)]


def gather(near, first, together):
    near, half = join(near), sum(len(p.offsets[0]) for p in near) // 2
    last = STAGES[2]
    ahead, behind = near.fetch(STAGES[1], 1), near.fetch(STAGES[1], -1)
    next_, prev = [near.fetch(last, 1)], [near.fetch(last, -1)]
    together([ahead, behind, next_[0], prev[0]])
    far_c = prev[0].fetch(last, -1)
    far_a = ahead.part(0, half).fetch(STAGES[1], 1)
    far_b = behind.part(half, 2 * half).fetch(STAGES[1], -1)
    one = join([ahead, behind])
    far_a, far_b, far_c = first([near, one], far_a, far_b, far_c)
    chunks = [near, one, join([far_a, far_b])]
    for chunk in chunks[1:]:
        next_.append(chunk.fetch(last, 1))
        prev.append(chunk.fetch(last, -1))
    if near.rows is not None:
        next_[1].rows, _ = lax.optimization_barrier((next_[1].rows, chunks[2].rows))
    far = [far_c, next_[1].fetch(last, 1), prev[2].fetch(last, -1)]
    return (
        chunks[:2],
        [chunks[2], next_[0], prev[0], far_c, next_[1], prev[1]],
        [next_[2], prev[2], *far[1:]],
    )


def row_ids(groups, here, local):
    packed = []
    for core in range(CORES):
        parts = []
        for group in groups:
            d = np.concatenate([p.offsets[core] for p in group], axis=0)
            x, y, z = d[:, 0] % XN, d[:, 1] % YN, d[:, 2] % ZN
            rel = (((x * YN + y) * ZN + z) * local + d[:, 3]).astype(np.int32)
            parts.append(np.pad(rel, (0, -len(rel) % LANES)))
        packed.append(np.concatenate(parts))
    d = jnp.where(here[3] == 0, jnp.asarray(packed[0]), jnp.asarray(packed[1]))
    r, d = d % local, d // local
    z, d = (here[2] + d % ZN) % ZN, d // ZN
    y, x = (here[1] + d % YN) % YN, (here[0] + d // YN) % XN
    return (flat_device(x, y, z, here[3]) * local + r).astype(jnp.float32)[None, :]


LANES = 128
BLOCK = 256


def score_kernel(scale, n, first, at, ids_ref, wanted_ref, other_wanted_ref, own_ref, other_ref, *refs):
    pieces, refs = refs[:n], refs[n:]
    if first:
        before, (mine, theirs, kept, arrived) = None, refs
        copy = pltpu.make_async_copy(other_ref, kept, arrived)
        copy.start()
    else:
        before, (mine, theirs), kept = refs[:2], refs[2:], other_ref
    count = own_ref.shape[0]
    rows = sum(piece.shape[0] for piece in pieces)
    whole = -(-rows // LANES) * LANES
    column = jnp.broadcast_to(ids_ref[0:1, at : at + whole], (LANES, whole)).T[:rows]
    ids = jnp.concatenate([column] * (BLOCK // LANES), axis=1)
    held = jnp.concatenate([piece[...] for piece in pieces], axis=0)
    for side, (particles, wanted, after) in enumerate(
        ((own_ref, wanted_ref, mine), (kept, other_wanted_ref, theirs))
    ):
        if first and side == 1:
            copy.wait()
        for start in range(0, count, BLOCK):
            cols = slice(start, start + BLOCK)
            block = particles[cols, :]
            want = wanted[0:1, cols]
            scores = scale * lax.dot_general(
                held, block, (((1,), (1,)), ((), ())), preferred_element_type=jnp.float32
            )
            top = jnp.max(scores, axis=0, keepdims=True)
            if not first:
                old_top = before[side][0:1, cols]
                top = jnp.maximum(top, old_top)
            total = jnp.sum(jnp.exp(scores - top), axis=0, keepdims=True)
            chosen = jnp.sum(jnp.where(ids == want, scores, 0.0), axis=0, keepdims=True)
            if not first:
                total = total + before[side][1:2, cols] * jnp.exp(old_top - top)
                chosen = chosen + before[side][2:3, cols]
            after[0:1, cols] = top
            after[1:2, cols] = total
            after[2:3, cols] = chosen


def score(pieces, ids, at, wanted, other_wanted, own, other, before, scale):
    count, voxels = own.shape
    rows = sum(p.rows.shape[0] for p in pieces)
    first = before is None
    whole = pl.BlockSpec(memory_space=pltpu.VMEM)
    operands = [ids, wanted, other_wanted, own, other, *(p.rows for p in pieces), *(before or ())]
    in_specs = [whole] * len(operands)
    out_shape = [jax.ShapeDtypeStruct((8, count), jnp.float32)] * 2
    if first:
        in_specs[4] = pl.BlockSpec(memory_space=pl.ANY)
        out_shape.append(jax.ShapeDtypeStruct(other.shape, other.dtype))
    return pl.pallas_call(
        functools.partial(score_kernel, scale, len(pieces), first, at),
        out_shape=out_shape,
        in_specs=in_specs,
        out_specs=[whole] * len(out_shape),
        scratch_shapes=[pltpu.SemaphoreType.DMA] if first else [],
        compiler_params=pltpu.CompilerParams(vmem_limit_bytes=16 << 20),
        cost_estimate=pl.CostEstimate(
            flops=4 * rows * count * voxels, transcendentals=2 * rows * count, bytes_accessed=rows * voxels * 2
        ),
        name="score",
    )(*operands)


def sums_kernel(classes, orients, key_ref, weights_ref, mine_ref, got_ref, particles_ref, out_ref):
    count, voxels = particles_ref.shape
    top = jnp.maximum(mine_ref[0:1, :], got_ref[0:1, :])
    total = mine_ref[1:2, :] * jnp.exp(mine_ref[0:1, :] - top) + got_ref[1:2, :] * jnp.exp(got_ref[0:1, :] - top)
    chosen = mine_ref[2:3, :] + got_ref[2:3, :]
    gain = weights_ref[...] * (classes * orients) * jnp.exp(chosen - top) / total
    steps = 2 * SHIFT + 1
    rows = lax.broadcasted_iota(jnp.int32, (steps * classes, count), 0)
    coef = jnp.where(rows == key_ref[...], gain, 0.0).astype(jnp.bfloat16)
    width = 512
    lane = lax.broadcasted_iota(jnp.int32, (classes, width), 1) % NX
    for base in range(0, voxels, width):
        moved = jnp.dot(coef, particles_ref[:, base : base + width], preferred_element_type=jnp.float32)
        summed = jnp.zeros((classes, width), jnp.float32)
        for k in range(steps):
            step = k - SHIFT
            part = moved[k * classes : (k + 1) * classes]
            if step != 0:
                inside = (lane >= step) if step > 0 else (lane < NX + step)
                wrapped = step - NX if step > 0 else step + NX
                part = jnp.where(
                    inside, pltpu.roll(part, step % width, 1), pltpu.roll(part, wrapped % width, 1)
                )
            summed = summed + part
        for j in range(width // LANES):
            out_ref[:, base // LANES + j, :] = summed[:, j * LANES : (j + 1) * LANES]


def class_sums(key, weights, mine, got, particles, classes, orients):
    count, voxels = particles.shape
    whole = pl.BlockSpec(memory_space=pltpu.VMEM)
    return pl.pallas_call(
        functools.partial(sums_kernel, classes, orients),
        out_shape=jax.ShapeDtypeStruct((classes, voxels // LANES, LANES), jnp.float32),
        in_specs=[whole] * 5,
        out_specs=whole,
        compiler_params=pltpu.CompilerParams(vmem_limit_bytes=16 << 20),
        name="class_sums",
    )(key, weights, mine, got, particles)


def body(references, particles, class_ids, orient_ids, offsets, weights):
    per_owner, local, voxels = references.shape
    devices = XN * YN * ZN * CORES
    classes = per_owner * XH * YN
    orients = local * XL * ZN * CORES
    count = particles.shape[0]
    scale = 1.0 / math.sqrt(voxels)
    xh, y, xl, z, core = (lax.axis_index(a) for a in ALL)
    here = (xh * XL + xl, y, z, core)

    other = swap_cores(particles)
    wanted = (class_ids * orients + orient_ids).astype(jnp.float32)[None, :]
    key = (class_ids + classes * (offsets + SHIFT))[None, :]
    other_wanted = swap_cores(wanted)

    start = np.zeros((local, 4), np.int32)
    start[:, 3] = np.arange(local)
    dry = gather(spread(Piece(None, [start, start])), lambda group, *halves: halves, lambda group: None)
    ids = row_ids(dry, here, local)
    near = spread(Piece(references.reshape(local, voxels), [start, start]))
    rows, ids, wanted, key = lax.optimization_barrier((near[-1].rows, ids, wanted, key))
    near[-1].rows = rows
    kept, stats, at = other, None, 0

    def take(group):
        nonlocal kept, stats, at
        out = score(group, ids, at, wanted, other_wanted, particles, kept, stats, scale)
        kept, stats = (out[2] if stats is None else kept), out[:2]
        count_rows = sum(len(p.offsets[0]) for p in group)
        at += -(-count_rows // LANES) * LANES

    def together(group):
        nonlocal kept
        *rows, kept = lax.optimization_barrier([p.rows for p in group] + [kept])
        for piece, there in zip(group, rows):
            piece.rows = there

    def first(group, *far):
        nonlocal stats
        take(group)
        *rows, stats = lax.optimization_barrier([p.rows for p in far] + [stats])
        for piece, there in zip(far, rows):
            piece.rows = there
        return far

    for group in gather(near, first, together)[1:]:
        take(group)
    mine, theirs = stats
    got = swap_cores(theirs)
    partial_sums = class_sums(key, weights[None, :], mine, got, particles, classes, orients)
    sent = partial_sums.reshape(devices, classes * voxels // devices)
    owned = jnp.sum(lax.all_to_all(sent, ALL, 0, 0, tiled=True), axis=0, keepdims=True)
    population = count * devices / classes
    return owned / jnp.sqrt(jnp.float32(population))


def solution(mesh):
    fine = Mesh(np.asarray(mesh.devices).reshape(XH, YN, XL, ZN, CORES), ALL)
    cls, ptl = ("xh", "y"), ("xl", "z", "core")
    placed = (P(cls, ptl, None), P(ALL, None), P(ALL), P(ALL), P(ALL), P(ALL))
    return jax.shard_map(
        body, mesh=fine, in_specs=placed, out_specs=P(cls, ptl), check_vma=False
    )
```

```python
import functools
import math

import jax
import jax.numpy as jnp
import numpy as np
from jax import lax
from jax.experimental import pallas as pl
from jax.experimental.pallas import tpu as pltpu
from jax.sharding import Mesh
from jax.sharding import PartitionSpec as P

NX = 64
SHIFT = 3
XH, YN, XL, ZN, CORES = 2, 4, 2, 8, 2
XN = XH * XL
ALL = ("xh", "y", "xl", "z", "core")
AX, AY, AZ = 0, 1, 2
SIZES = (XN, YN, ZN)
STAGES = ((AX, AZ), (AY, AY), (AZ, AX))


def flat_device(x, y, z, core):
    return (((x // XL * YN + y) * XL + x % XL) * ZN + z) * CORES + core


def pairs(move):
    out = []
    for x in range(XN):
        for y in range(YN):
            for z in range(ZN):
                for core in range(CORES):
                    (tx, ty, tz), tc = move([x, y, z], core)
                    out.append((flat_device(x, y, z, core), flat_device(tx % XN, ty % YN, tz % ZN, tc)))
    return out


def swap_cores(value):
    return lax.ppermute(value, ALL, pairs(lambda at, core: (at, 1 - core)))


class Piece:
    def __init__(self, rows, offsets):
        self.rows, self.offsets = rows, offsets

    def part(self, start, stop):
        rows = None if self.rows is None else self.rows[start:stop]
        return Piece(rows, [o[start:stop] for o in self.offsets])

    def fetch(self, axes, steps):
        def move(at, core):
            at[axes[core]] -= steps
            return at, core

        moved = [o + steps * np.eye(4, dtype=np.int32)[axis] for o, axis in zip(self.offsets, axes)]
        rows = None if self.rows is None else lax.ppermute(self.rows, ALL, pairs(move))
        return Piece(rows, moved)


def join(pieces):
    rows = None if pieces[0].rows is None else jnp.concatenate([p.rows for p in pieces], axis=0)
    offsets = [np.concatenate([p.offsets[c] for p in pieces], axis=0) for c in range(CORES)]
    return Piece(rows, offsets)


def spread(piece):
    piece = join([piece, piece.fetch((AZ, AZ), ZN // 2)])
    return [piece] + [piece.fetch(STAGES[0], steps) for steps in (1, -1, 2)]


def gather(near, first, together):
    near, half = join(near), sum(len(p.offsets[0]) for p in near) // 2
    last = STAGES[2]
    ahead, behind = near.fetch(STAGES[1], 1), near.fetch(STAGES[1], -1)
    next_, prev = [near.fetch(last, 1)], [near.fetch(last, -1)]
    together([ahead, behind, next_[0], prev[0]])
    far_c = prev[0].fetch(last, -1)
    far_a = ahead.part(0, half).fetch(STAGES[1], 1)
    far_b = behind.part(half, 2 * half).fetch(STAGES[1], -1)
    one = join([ahead, behind])
    far_a, far_b, far_c = first([near, one], far_a, far_b, far_c)
    chunks = [near, one, join([far_a, far_b])]
    for chunk in chunks[1:]:
        next_.append(chunk.fetch(last, 1))
        prev.append(chunk.fetch(last, -1))
    side_a, side_b = far_c.fetch(STAGES[1], 1), far_c.fetch(STAGES[1], -1)
    far = [
        side_a,
        side_b,
        side_a.part(0, half).fetch(STAGES[1], 1),
        side_b.part(half, 2 * half).fetch(STAGES[1], -1),
    ]
    return (
        chunks[:2],
        [chunks[2], next_[0], prev[0], far_c, next_[1], prev[1]],
        [next_[2], prev[2], *far],
    )


def row_ids(groups, here, local):
    packed = []
    for core in range(CORES):
        parts = []
        for group in groups:
            d = np.concatenate([p.offsets[core] for p in group], axis=0)
            x, y, z = d[:, 0] % XN, d[:, 1] % YN, d[:, 2] % ZN
            rel = (((x * YN + y) * ZN + z) * local + d[:, 3]).astype(np.int32)
            parts.append(np.pad(rel, (0, -len(rel) % LANES)))
        packed.append(np.concatenate(parts))
    d = jnp.where(here[3] == 0, jnp.asarray(packed[0]), jnp.asarray(packed[1]))
    r, d = d % local, d // local
    z, d = (here[2] + d % ZN) % ZN, d // ZN
    y, x = (here[1] + d % YN) % YN, (here[0] + d // YN) % XN
    return (flat_device(x, y, z, here[3]) * local + r).astype(jnp.float32)[None, :]


LANES = 128
BLOCK = 256


def score_kernel(scale, n, first, at, ids_ref, wanted_ref, other_wanted_ref, own_ref, other_ref, *refs):
    pieces, refs = refs[:n], refs[n:]
    if first:
        before, (mine, theirs, kept, arrived) = None, refs
        copy = pltpu.make_async_copy(other_ref, kept, arrived)
        copy.start()
    else:
        before, (mine, theirs), kept = refs[:2], refs[2:], other_ref
    count = own_ref.shape[0]
    rows = sum(piece.shape[0] for piece in pieces)
    whole = -(-rows // LANES) * LANES
    column = jnp.broadcast_to(ids_ref[0:1, at : at + whole], (LANES, whole)).T[:rows]
    ids = jnp.concatenate([column] * (BLOCK // LANES), axis=1)
    held = jnp.concatenate([piece[...] for piece in pieces], axis=0)
    for side, (particles, wanted, after) in enumerate(
        ((own_ref, wanted_ref, mine), (kept, other_wanted_ref, theirs))
    ):
        if first and side == 1:
            copy.wait()
        for start in range(0, count, BLOCK):
            cols = slice(start, start + BLOCK)
            block = particles[cols, :]
            want = wanted[0:1, cols]
            scores = scale * lax.dot_general(
                held, block, (((1,), (1,)), ((), ())), preferred_element_type=jnp.float32
            )
            top = jnp.max(scores, axis=0, keepdims=True)
            if not first:
                old_top = before[side][0:1, cols]
                top = jnp.maximum(top, old_top)
            total = jnp.sum(jnp.exp(scores - top), axis=0, keepdims=True)
            chosen = jnp.sum(jnp.where(ids == want, scores, 0.0), axis=0, keepdims=True)
            if not first:
                total = total + before[side][1:2, cols] * jnp.exp(old_top - top)
                chosen = chosen + before[side][2:3, cols]
            after[0:1, cols] = top
            after[1:2, cols] = total
            after[2:3, cols] = chosen


def score(pieces, ids, at, wanted, other_wanted, own, other, before, scale):
    count, voxels = own.shape
    rows = sum(p.rows.shape[0] for p in pieces)
    first = before is None
    whole = pl.BlockSpec(memory_space=pltpu.VMEM)
    operands = [ids, wanted, other_wanted, own, other, *(p.rows for p in pieces), *(before or ())]
    in_specs = [whole] * len(operands)
    out_shape = [jax.ShapeDtypeStruct((8, count), jnp.float32)] * 2
    if first:
        in_specs[4] = pl.BlockSpec(memory_space=pl.ANY)
        out_shape.append(jax.ShapeDtypeStruct(other.shape, other.dtype))
    return pl.pallas_call(
        functools.partial(score_kernel, scale, len(pieces), first, at),
        out_shape=out_shape,
        in_specs=in_specs,
        out_specs=[whole] * len(out_shape),
        scratch_shapes=[pltpu.SemaphoreType.DMA] if first else [],
        compiler_params=pltpu.CompilerParams(vmem_limit_bytes=16 << 20),
        cost_estimate=pl.CostEstimate(
            flops=4 * rows * count * voxels, transcendentals=2 * rows * count, bytes_accessed=rows * voxels * 2
        ),
        name="score",
    )(*operands)


def sums_kernel(classes, orients, key_ref, weights_ref, mine_ref, got_ref, particles_ref, out_ref):
    count, voxels = particles_ref.shape
    top = jnp.maximum(mine_ref[0:1, :], got_ref[0:1, :])
    total = mine_ref[1:2, :] * jnp.exp(mine_ref[0:1, :] - top) + got_ref[1:2, :] * jnp.exp(got_ref[0:1, :] - top)
    chosen = mine_ref[2:3, :] + got_ref[2:3, :]
    gain = weights_ref[...] * (classes * orients) * jnp.exp(chosen - top) / total
    steps = 2 * SHIFT + 1
    rows = lax.broadcasted_iota(jnp.int32, (steps * classes, count), 0)
    coef = jnp.where(rows == key_ref[...], gain, 0.0).astype(jnp.bfloat16)
    width = 512
    lane = lax.broadcasted_iota(jnp.int32, (classes, width), 1) % NX
    for base in range(0, voxels, width):
        moved = jnp.dot(coef, particles_ref[:, base : base + width], preferred_element_type=jnp.float32)
        summed = jnp.zeros((classes, width), jnp.float32)
        for k in range(steps):
            step = k - SHIFT
            part = moved[k * classes : (k + 1) * classes]
            if step != 0:
                inside = (lane >= step) if step > 0 else (lane < NX + step)
                wrapped = step - NX if step > 0 else step + NX
                part = jnp.where(
                    inside, pltpu.roll(part, step % width, 1), pltpu.roll(part, wrapped % width, 1)
                )
            summed = summed + part
        for j in range(width // LANES):
            out_ref[:, base // LANES + j, :] = summed[:, j * LANES : (j + 1) * LANES]


def class_sums(key, weights, mine, got, particles, classes, orients):
    count, voxels = particles.shape
    whole = pl.BlockSpec(memory_space=pltpu.VMEM)
    return pl.pallas_call(
        functools.partial(sums_kernel, classes, orients),
        out_shape=jax.ShapeDtypeStruct((classes, voxels // LANES, LANES), jnp.float32),
        in_specs=[whole] * 5,
        out_specs=whole,
        compiler_params=pltpu.CompilerParams(vmem_limit_bytes=16 << 20),
        name="class_sums",
    )(key, weights, mine, got, particles)


def body(references, particles, class_ids, orient_ids, offsets, weights):
    per_owner, local, voxels = references.shape
    devices = XN * YN * ZN * CORES
    classes = per_owner * XH * YN
    orients = local * XL * ZN * CORES
    count = particles.shape[0]
    scale = 1.0 / math.sqrt(voxels)
    xh, y, xl, z, core = (lax.axis_index(a) for a in ALL)
    here = (xh * XL + xl, y, z, core)

    other = swap_cores(particles)
    wanted = (class_ids * orients + orient_ids).astype(jnp.float32)[None, :]
    key = (class_ids + classes * (offsets + SHIFT))[None, :]
    other_wanted = swap_cores(wanted)

    start = np.zeros((local, 4), np.int32)
    start[:, 3] = np.arange(local)
    dry = gather(spread(Piece(None, [start, start])), lambda group, *halves: halves, lambda group: None)
    ids = row_ids(dry, here, local)
    near = spread(Piece(references.reshape(local, voxels), [start, start]))
    rows, ids, wanted, key = lax.optimization_barrier((near[-1].rows, ids, wanted, key))
    near[-1].rows = rows
    kept, stats, at = other, None, 0

    def take(group):
        nonlocal kept, stats, at
        out = score(group, ids, at, wanted, other_wanted, particles, kept, stats, scale)
        kept, stats = (out[2] if stats is None else kept), out[:2]
        count_rows = sum(len(p.offsets[0]) for p in group)
        at += -(-count_rows // LANES) * LANES

    def together(group):
        nonlocal kept
        *rows, kept = lax.optimization_barrier([p.rows for p in group] + [kept])
        for piece, there in zip(group, rows):
            piece.rows = there

    def first(group, *far):
        nonlocal stats
        take(group)
        *rows, stats = lax.optimization_barrier([p.rows for p in far] + [stats])
        for piece, there in zip(far, rows):
            piece.rows = there
        return far

    for group in gather(near, first, together)[1:]:
        take(group)
    mine, theirs = stats
    got = swap_cores(theirs)
    partial_sums = class_sums(key, weights[None, :], mine, got, particles, classes, orients)
    sent = partial_sums.reshape(devices, classes * voxels // devices)
    owned = jnp.sum(lax.all_to_all(sent, ALL, 0, 0, tiled=True), axis=0, keepdims=True)
    population = count * devices / classes
    return owned / jnp.sqrt(jnp.float32(population))


def solution(mesh):
    fine = Mesh(np.asarray(mesh.devices).reshape(XH, YN, XL, ZN, CORES), ALL)
    cls, ptl = ("xh", "y"), ("xl", "z", "core")
    placed = (P(cls, ptl, None), P(ALL, None), P(ALL), P(ALL), P(ALL), P(ALL))
    return jax.shard_map(
        body, mesh=fine, in_specs=placed, out_specs=P(cls, ptl), check_vma=False
    )
```

```python
import functools
import math

import jax
import jax.numpy as jnp
import numpy as np
from jax import lax
from jax.experimental import pallas as pl
from jax.experimental.pallas import tpu as pltpu
from jax.sharding import Mesh
from jax.sharding import PartitionSpec as P

NX = 64
SHIFT = 3
XH, YN, XL, ZN, CORES = 2, 4, 2, 8, 2
XN = XH * XL
ALL = ("xh", "y", "xl", "z", "core")
AX, AY, AZ = 0, 1, 2
SIZES = (XN, YN, ZN)
STAGES = ((AX, AZ), (AY, AY), (AZ, AX))


def flat_device(x, y, z, core):
    return (((x // XL * YN + y) * XL + x % XL) * ZN + z) * CORES + core


def pairs(move):
    out = []
    for x in range(XN):
        for y in range(YN):
            for z in range(ZN):
                for core in range(CORES):
                    (tx, ty, tz), tc = move([x, y, z], core)
                    out.append((flat_device(x, y, z, core), flat_device(tx % XN, ty % YN, tz % ZN, tc)))
    return out


def swap_cores(value):
    return lax.ppermute(value, ALL, pairs(lambda at, core: (at, 1 - core)))


class Piece:
    def __init__(self, rows, offsets):
        self.rows, self.offsets = rows, offsets

    def part(self, start, stop):
        rows = None if self.rows is None else self.rows[start:stop]
        return Piece(rows, [o[start:stop] for o in self.offsets])

    def fetch(self, axes, steps):
        def move(at, core):
            at[axes[core]] -= steps
            return at, core

        moved = [o + steps * np.eye(4, dtype=np.int32)[axis] for o, axis in zip(self.offsets, axes)]
        rows = None if self.rows is None else lax.ppermute(self.rows, ALL, pairs(move))
        return Piece(rows, moved)


def join(pieces):
    rows = None if pieces[0].rows is None else jnp.concatenate([p.rows for p in pieces], axis=0)
    offsets = [np.concatenate([p.offsets[c] for p in pieces], axis=0) for c in range(CORES)]
    return Piece(rows, offsets)


def spread(piece):
    piece = join([piece, piece.fetch((AZ, AZ), ZN // 2)])
    return [piece] + [piece.fetch(STAGES[0], steps) for steps in (1, -1, 2)]


def gather(near, first, together):
    near, half = join(near), sum(len(p.offsets[0]) for p in near) // 2
    last = STAGES[2]
    ahead, behind = near.fetch(STAGES[1], 1), near.fetch(STAGES[1], -1)
    next_, prev = [near.fetch(last, 1)], [near.fetch(last, -1)]
    together([ahead, next_[0], prev[0]])
    far_c = prev[0].fetch(last, -1)
    far_a = ahead.part(0, half).fetch(STAGES[1], 1)
    far_b = behind.part(half, 2 * half).fetch(STAGES[1], -1)
    one = join([ahead, behind])
    far_a, far_b, far_c = first([near, one], far_a, far_b, far_c)
    chunks = [near, one, join([far_a, far_b])]
    for chunk in chunks[1:]:
        next_.append(chunk.fetch(last, 1))
        prev.append(chunk.fetch(last, -1))
    side_a, side_b = far_c.fetch(STAGES[1], 1), far_c.fetch(STAGES[1], -1)
    far = [
        side_a,
        side_b,
        side_a.part(0, half).fetch(STAGES[1], 1),
        side_b.part(half, 2 * half).fetch(STAGES[1], -1),
    ]
    return (
        chunks[:2],
        [chunks[2], next_[0], prev[0], far_c, next_[1], prev[1]],
        [next_[2], prev[2], *far],
    )


def row_ids(groups, here, local):
    packed = []
    for core in range(CORES):
        parts = []
        for group in groups:
            d = np.concatenate([p.offsets[core] for p in group], axis=0)
            x, y, z = d[:, 0] % XN, d[:, 1] % YN, d[:, 2] % ZN
            rel = (((x * YN + y) * ZN + z) * local + d[:, 3]).astype(np.int32)
            parts.append(np.pad(rel, (0, -len(rel) % LANES)))
        packed.append(np.concatenate(parts))
    d = jnp.where(here[3] == 0, jnp.asarray(packed[0]), jnp.asarray(packed[1]))
    r, d = d % local, d // local
    z, d = (here[2] + d % ZN) % ZN, d // ZN
    y, x = (here[1] + d % YN) % YN, (here[0] + d // YN) % XN
    return (flat_device(x, y, z, here[3]) * local + r).astype(jnp.float32)[None, :]


LANES = 128
BLOCK = 256


def score_kernel(scale, n, first, at, ids_ref, wanted_ref, other_wanted_ref, own_ref, other_ref, *refs):
    pieces, refs = refs[:n], refs[n:]
    if first:
        before, (mine, theirs, kept, arrived) = None, refs
        copy = pltpu.make_async_copy(other_ref, kept, arrived)
        copy.start()
    else:
        before, (mine, theirs), kept = refs[:2], refs[2:], other_ref
    count = own_ref.shape[0]
    rows = sum(piece.shape[0] for piece in pieces)
    whole = -(-rows // LANES) * LANES
    column = jnp.broadcast_to(ids_ref[0:1, at : at + whole], (LANES, whole)).T[:rows]
    ids = jnp.concatenate([column] * (BLOCK // LANES), axis=1)
    held = jnp.concatenate([piece[...] for piece in pieces], axis=0)
    for side, (particles, wanted, after) in enumerate(
        ((own_ref, wanted_ref, mine), (kept, other_wanted_ref, theirs))
    ):
        if first and side == 1:
            copy.wait()
        for start in range(0, count, BLOCK):
            cols = slice(start, start + BLOCK)
            block = particles[cols, :]
            want = wanted[0:1, cols]
            scores = scale * lax.dot_general(
                held, block, (((1,), (1,)), ((), ())), preferred_element_type=jnp.float32
            )
            top = jnp.max(scores, axis=0, keepdims=True)
            if not first:
                old_top = before[side][0:1, cols]
                top = jnp.maximum(top, old_top)
            total = jnp.sum(jnp.exp(scores - top), axis=0, keepdims=True)
            chosen = jnp.sum(jnp.where(ids == want, scores, 0.0), axis=0, keepdims=True)
            if not first:
                total = total + before[side][1:2, cols] * jnp.exp(old_top - top)
                chosen = chosen + before[side][2:3, cols]
            after[0:1, cols] = top
            after[1:2, cols] = total
            after[2:3, cols] = chosen


def score(pieces, ids, at, wanted, other_wanted, own, other, before, scale):
    count, voxels = own.shape
    rows = sum(p.rows.shape[0] for p in pieces)
    first = before is None
    whole = pl.BlockSpec(memory_space=pltpu.VMEM)
    operands = [ids, wanted, other_wanted, own, other, *(p.rows for p in pieces), *(before or ())]
    in_specs = [whole] * len(operands)
    out_shape = [jax.ShapeDtypeStruct((8, count), jnp.float32)] * 2
    if first:
        in_specs[4] = pl.BlockSpec(memory_space=pl.ANY)
        out_shape.append(jax.ShapeDtypeStruct(other.shape, other.dtype))
    return pl.pallas_call(
        functools.partial(score_kernel, scale, len(pieces), first, at),
        out_shape=out_shape,
        in_specs=in_specs,
        out_specs=[whole] * len(out_shape),
        scratch_shapes=[pltpu.SemaphoreType.DMA] if first else [],
        compiler_params=pltpu.CompilerParams(vmem_limit_bytes=16 << 20),
        cost_estimate=pl.CostEstimate(
            flops=4 * rows * count * voxels, transcendentals=2 * rows * count, bytes_accessed=rows * voxels * 2
        ),
        name="score",
    )(*operands)


def sums_kernel(classes, orients, key_ref, weights_ref, mine_ref, got_ref, particles_ref, out_ref):
    count, voxels = particles_ref.shape
    top = jnp.maximum(mine_ref[0:1, :], got_ref[0:1, :])
    total = mine_ref[1:2, :] * jnp.exp(mine_ref[0:1, :] - top) + got_ref[1:2, :] * jnp.exp(got_ref[0:1, :] - top)
    chosen = mine_ref[2:3, :] + got_ref[2:3, :]
    gain = weights_ref[...] * (classes * orients) * jnp.exp(chosen - top) / total
    steps = 2 * SHIFT + 1
    rows = lax.broadcasted_iota(jnp.int32, (steps * classes, count), 0)
    coef = jnp.where(rows == key_ref[...], gain, 0.0).astype(jnp.bfloat16)
    width = 512
    lane = lax.broadcasted_iota(jnp.int32, (classes, width), 1) % NX
    for base in range(0, voxels, width):
        moved = jnp.dot(coef, particles_ref[:, base : base + width], preferred_element_type=jnp.float32)
        summed = jnp.zeros((classes, width), jnp.float32)
        for k in range(steps):
            step = k - SHIFT
            part = moved[k * classes : (k + 1) * classes]
            if step != 0:
                inside = (lane >= step) if step > 0 else (lane < NX + step)
                wrapped = step - NX if step > 0 else step + NX
                part = jnp.where(
                    inside, pltpu.roll(part, step % width, 1), pltpu.roll(part, wrapped % width, 1)
                )
            summed = summed + part
        for j in range(width // LANES):
            out_ref[:, base // LANES + j, :] = summed[:, j * LANES : (j + 1) * LANES]


def class_sums(key, weights, mine, got, particles, classes, orients):
    count, voxels = particles.shape
    whole = pl.BlockSpec(memory_space=pltpu.VMEM)
    return pl.pallas_call(
        functools.partial(sums_kernel, classes, orients),
        out_shape=jax.ShapeDtypeStruct((classes, voxels // LANES, LANES), jnp.float32),
        in_specs=[whole] * 5,
        out_specs=whole,
        compiler_params=pltpu.CompilerParams(vmem_limit_bytes=16 << 20),
        name="class_sums",
    )(key, weights, mine, got, particles)


def body(references, particles, class_ids, orient_ids, offsets, weights):
    per_owner, local, voxels = references.shape
    devices = XN * YN * ZN * CORES
    classes = per_owner * XH * YN
    orients = local * XL * ZN * CORES
    count = particles.shape[0]
    scale = 1.0 / math.sqrt(voxels)
    xh, y, xl, z, core = (lax.axis_index(a) for a in ALL)
    here = (xh * XL + xl, y, z, core)

    other = swap_cores(particles)
    wanted = (class_ids * orients + orient_ids).astype(jnp.float32)[None, :]
    key = (class_ids + classes * (offsets + SHIFT))[None, :]
    other_wanted = swap_cores(wanted)

    start = np.zeros((local, 4), np.int32)
    start[:, 3] = np.arange(local)
    dry = gather(spread(Piece(None, [start, start])), lambda group, *halves: halves, lambda group: None)
    ids = row_ids(dry, here, local)
    near = spread(Piece(references.reshape(local, voxels), [start, start]))
    rows, ids, wanted, key = lax.optimization_barrier((near[-1].rows, ids, wanted, key))
    near[-1].rows = rows
    kept, stats, at = other, None, 0

    def take(group):
        nonlocal kept, stats, at
        out = score(group, ids, at, wanted, other_wanted, particles, kept, stats, scale)
        kept, stats = (out[2] if stats is None else kept), out[:2]
        count_rows = sum(len(p.offsets[0]) for p in group)
        at += -(-count_rows // LANES) * LANES

    def together(group):
        nonlocal kept
        *rows, kept = lax.optimization_barrier([p.rows for p in group] + [kept])
        for piece, there in zip(group, rows):
            piece.rows = there

    def first(group, *far):
        nonlocal stats
        take(group)
        *rows, stats = lax.optimization_barrier([p.rows for p in far] + [stats])
        for piece, there in zip(far, rows):
            piece.rows = there
        return far

    for group in gather(near, first, together)[1:]:
        take(group)
    mine, theirs = stats
    got = swap_cores(theirs)
    partial_sums = class_sums(key, weights[None, :], mine, got, particles, classes, orients)
    sent = partial_sums.reshape(devices, classes * voxels // devices)
    owned = jnp.sum(lax.all_to_all(sent, ALL, 0, 0, tiled=True), axis=0, keepdims=True)
    population = count * devices / classes
    return owned / jnp.sqrt(jnp.float32(population))


def solution(mesh):
    fine = Mesh(np.asarray(mesh.devices).reshape(XH, YN, XL, ZN, CORES), ALL)
    cls, ptl = ("xh", "y"), ("xl", "z", "core")
    placed = (P(cls, ptl, None), P(ALL, None), P(ALL), P(ALL), P(ALL), P(ALL))
    return jax.shard_map(
        body, mesh=fine, in_specs=placed, out_specs=P(cls, ptl), check_vma=False
    )
```

```python
import functools
import math

import jax
import jax.numpy as jnp
import numpy as np
from jax import lax
from jax.experimental import pallas as pl
from jax.experimental.pallas import tpu as pltpu
from jax.sharding import Mesh
from jax.sharding import PartitionSpec as P

NX = 64
SHIFT = 3
XH, YN, XL, ZN, CORES = 2, 4, 2, 8, 2
XN = XH * XL
ALL = ("xh", "y", "xl", "z", "core")
AX, AY, AZ = 0, 1, 2
SIZES = (XN, YN, ZN)
STAGES = ((AY, AX), (AZ, AZ), (AX, AY))


def flat_device(x, y, z, core):
    return (((x // XL * YN + y) * XL + x % XL) * ZN + z) * CORES + core


def pairs(move):
    out = []
    for x in range(XN):
        for y in range(YN):
            for z in range(ZN):
                for core in range(CORES):
                    (tx, ty, tz), tc = move([x, y, z], core)
                    out.append((flat_device(x, y, z, core), flat_device(tx % XN, ty % YN, tz % ZN, tc)))
    return out


def swap_cores(value):
    return lax.ppermute(value, ALL, pairs(lambda at, core: (at, 1 - core)))


class Piece:
    def __init__(self, rows, offsets):
        self.rows, self.offsets = rows, offsets

    def part(self, start, stop):
        rows = None if self.rows is None else self.rows[start:stop]
        return Piece(rows, [o[start:stop] for o in self.offsets])

    def fetch(self, axes, steps):
        def move(at, core):
            at[axes[core]] -= steps
            return at, core

        moved = [o + steps * np.eye(4, dtype=np.int32)[axis] for o, axis in zip(self.offsets, axes)]
        rows = None if self.rows is None else lax.ppermute(self.rows, ALL, pairs(move))
        return Piece(rows, moved)


def join(pieces):
    rows = None if pieces[0].rows is None else jnp.concatenate([p.rows for p in pieces], axis=0)
    offsets = [np.concatenate([p.offsets[c] for p in pieces], axis=0) for c in range(CORES)]
    return Piece(rows, offsets)


def spread(piece):
    piece = join([piece, piece.fetch((AZ, AZ), ZN // 2)])
    return [piece] + [piece.fetch(STAGES[0], steps) for steps in (1, -1, 2)]


def gather(near, first, together):
    near, half = join(near), sum(len(p.offsets[0]) for p in near) // 2
    last = STAGES[2]
    ahead, behind = near.fetch(STAGES[1], 1), near.fetch(STAGES[1], -1)
    next_, prev = [near.fetch(last, 1)], [near.fetch(last, -1)]
    together([ahead, next_[0], prev[0]])
    far_c = prev[0].fetch(last, -1)
    far_a = ahead.part(0, half).fetch(STAGES[1], 1)
    far_b = behind.part(half, 2 * half).fetch(STAGES[1], -1)
    one = join([ahead, behind])
    far_a, far_b, far_c = first([near, one], far_a, far_b, far_c)
    chunks = [near, one, join([far_a, far_b])]
    for chunk in chunks[1:]:
        next_.append(chunk.fetch(last, 1))
        prev.append(chunk.fetch(last, -1))
    side_a, side_b = far_c.fetch(STAGES[1], 1), far_c.fetch(STAGES[1], -1)
    far = [
        side_a,
        side_b,
        side_a.part(0, half).fetch(STAGES[1], 1),
        side_b.part(half, 2 * half).fetch(STAGES[1], -1),
    ]
    return (
        chunks[:2],
        [chunks[2], next_[0], prev[0], far_c, next_[1], prev[1]],
        [next_[2], prev[2], *far],
    )


def row_ids(groups, here, local):
    packed = []
    for core in range(CORES):
        parts = []
        for group in groups:
            d = np.concatenate([p.offsets[core] for p in group], axis=0)
            x, y, z = d[:, 0] % XN, d[:, 1] % YN, d[:, 2] % ZN
            rel = (((x * YN + y) * ZN + z) * local + d[:, 3]).astype(np.int32)
            parts.append(np.pad(rel, (0, -len(rel) % LANES)))
        packed.append(np.concatenate(parts))
    d = jnp.where(here[3] == 0, jnp.asarray(packed[0]), jnp.asarray(packed[1]))
    r, d = d % local, d // local
    z, d = (here[2] + d % ZN) % ZN, d // ZN
    y, x = (here[1] + d % YN) % YN, (here[0] + d // YN) % XN
    return (flat_device(x, y, z, here[3]) * local + r).astype(jnp.float32)[None, :]


LANES = 128
BLOCK = 256


def score_kernel(scale, n, first, at, ids_ref, wanted_ref, other_wanted_ref, own_ref, other_ref, *refs):
    pieces, refs = refs[:n], refs[n:]
    if first:
        before, (mine, theirs, kept, arrived) = None, refs
        copy = pltpu.make_async_copy(other_ref, kept, arrived)
        copy.start()
    else:
        before, (mine, theirs), kept = refs[:2], refs[2:], other_ref
    count = own_ref.shape[0]
    rows = sum(piece.shape[0] for piece in pieces)
    whole = -(-rows // LANES) * LANES
    column = jnp.broadcast_to(ids_ref[0:1, at : at + whole], (LANES, whole)).T[:rows]
    ids = jnp.concatenate([column] * (BLOCK // LANES), axis=1)
    held = jnp.concatenate([piece[...] for piece in pieces], axis=0)
    for side, (particles, wanted, after) in enumerate(
        ((own_ref, wanted_ref, mine), (kept, other_wanted_ref, theirs))
    ):
        if first and side == 1:
            copy.wait()
        for start in range(0, count, BLOCK):
            cols = slice(start, start + BLOCK)
            block = particles[cols, :]
            want = wanted[0:1, cols]
            scores = scale * lax.dot_general(
                held, block, (((1,), (1,)), ((), ())), preferred_element_type=jnp.float32
            )
            top = jnp.max(scores, axis=0, keepdims=True)
            if not first:
                old_top = before[side][0:1, cols]
                top = jnp.maximum(top, old_top)
            total = jnp.sum(jnp.exp(scores - top), axis=0, keepdims=True)
            chosen = jnp.sum(jnp.where(ids == want, scores, 0.0), axis=0, keepdims=True)
            if not first:
                total = total + before[side][1:2, cols] * jnp.exp(old_top - top)
                chosen = chosen + before[side][2:3, cols]
            after[0:1, cols] = top
            after[1:2, cols] = total
            after[2:3, cols] = chosen


def score(pieces, ids, at, wanted, other_wanted, own, other, before, scale):
    count, voxels = own.shape
    rows = sum(p.rows.shape[0] for p in pieces)
    first = before is None
    whole = pl.BlockSpec(memory_space=pltpu.VMEM)
    operands = [ids, wanted, other_wanted, own, other, *(p.rows for p in pieces), *(before or ())]
    in_specs = [whole] * len(operands)
    out_shape = [jax.ShapeDtypeStruct((8, count), jnp.float32)] * 2
    if first:
        in_specs[4] = pl.BlockSpec(memory_space=pl.ANY)
        out_shape.append(jax.ShapeDtypeStruct(other.shape, other.dtype))
    return pl.pallas_call(
        functools.partial(score_kernel, scale, len(pieces), first, at),
        out_shape=out_shape,
        in_specs=in_specs,
        out_specs=[whole] * len(out_shape),
        scratch_shapes=[pltpu.SemaphoreType.DMA] if first else [],
        compiler_params=pltpu.CompilerParams(vmem_limit_bytes=16 << 20),
        cost_estimate=pl.CostEstimate(
            flops=4 * rows * count * voxels, transcendentals=2 * rows * count, bytes_accessed=rows * voxels * 2
        ),
        name="score",
    )(*operands)


def sums_kernel(classes, orients, key_ref, weights_ref, mine_ref, got_ref, particles_ref, out_ref):
    count, voxels = particles_ref.shape
    top = jnp.maximum(mine_ref[0:1, :], got_ref[0:1, :])
    total = mine_ref[1:2, :] * jnp.exp(mine_ref[0:1, :] - top) + got_ref[1:2, :] * jnp.exp(got_ref[0:1, :] - top)
    chosen = mine_ref[2:3, :] + got_ref[2:3, :]
    gain = weights_ref[...] * (classes * orients) * jnp.exp(chosen - top) / total
    steps = 2 * SHIFT + 1
    rows = lax.broadcasted_iota(jnp.int32, (steps * classes, count), 0)
    coef = jnp.where(rows == key_ref[...], gain, 0.0).astype(jnp.bfloat16)
    width = 512
    lane = lax.broadcasted_iota(jnp.int32, (classes, width), 1) % NX
    for base in range(0, voxels, width):
        moved = jnp.dot(coef, particles_ref[:, base : base + width], preferred_element_type=jnp.float32)
        summed = jnp.zeros((classes, width), jnp.float32)
        for k in range(steps):
            step = k - SHIFT
            part = moved[k * classes : (k + 1) * classes]
            if step != 0:
                inside = (lane >= step) if step > 0 else (lane < NX + step)
                wrapped = step - NX if step > 0 else step + NX
                part = jnp.where(
                    inside, pltpu.roll(part, step % width, 1), pltpu.roll(part, wrapped % width, 1)
                )
            summed = summed + part
        for j in range(width // LANES):
            out_ref[:, base // LANES + j, :] = summed[:, j * LANES : (j + 1) * LANES]


def class_sums(key, weights, mine, got, particles, classes, orients):
    count, voxels = particles.shape
    whole = pl.BlockSpec(memory_space=pltpu.VMEM)
    return pl.pallas_call(
        functools.partial(sums_kernel, classes, orients),
        out_shape=jax.ShapeDtypeStruct((classes, voxels // LANES, LANES), jnp.float32),
        in_specs=[whole] * 5,
        out_specs=whole,
        compiler_params=pltpu.CompilerParams(vmem_limit_bytes=16 << 20),
        name="class_sums",
    )(key, weights, mine, got, particles)


def body(references, particles, class_ids, orient_ids, offsets, weights):
    per_owner, local, voxels = references.shape
    devices = XN * YN * ZN * CORES
    classes = per_owner * XH * YN
    orients = local * XL * ZN * CORES
    count = particles.shape[0]
    scale = 1.0 / math.sqrt(voxels)
    xh, y, xl, z, core = (lax.axis_index(a) for a in ALL)
    here = (xh * XL + xl, y, z, core)

    other = swap_cores(particles)
    wanted = (class_ids * orients + orient_ids).astype(jnp.float32)[None, :]
    key = (class_ids + classes * (offsets + SHIFT))[None, :]
    other_wanted = swap_cores(wanted)

    start = np.zeros((local, 4), np.int32)
    start[:, 3] = np.arange(local)
    dry = gather(spread(Piece(None, [start, start])), lambda group, *halves: halves, lambda group: None)
    ids = row_ids(dry, here, local)
    near = spread(Piece(references.reshape(local, voxels), [start, start]))
    rows, ids, wanted, key = lax.optimization_barrier((near[-1].rows, ids, wanted, key))
    near[-1].rows = rows
    kept, stats, at = other, None, 0

    def take(group):
        nonlocal kept, stats, at
        out = score(group, ids, at, wanted, other_wanted, particles, kept, stats, scale)
        kept, stats = (out[2] if stats is None else kept), out[:2]
        count_rows = sum(len(p.offsets[0]) for p in group)
        at += -(-count_rows // LANES) * LANES

    def together(group):
        nonlocal kept
        *rows, kept = lax.optimization_barrier([p.rows for p in group] + [kept])
        for piece, there in zip(group, rows):
            piece.rows = there

    def first(group, *far):
        nonlocal stats
        take(group)
        *rows, stats = lax.optimization_barrier([p.rows for p in far] + [stats])
        for piece, there in zip(far, rows):
            piece.rows = there
        return far

    for group in gather(near, first, together)[1:]:
        take(group)
    mine, theirs = stats
    got = swap_cores(theirs)
    partial_sums = class_sums(key, weights[None, :], mine, got, particles, classes, orients)
    sent = partial_sums.reshape(devices, classes * voxels // devices)
    owned = jnp.sum(lax.all_to_all(sent, ALL, 0, 0, tiled=True), axis=0, keepdims=True)
    population = count * devices / classes
    return owned / jnp.sqrt(jnp.float32(population))


def solution(mesh):
    fine = Mesh(np.asarray(mesh.devices).reshape(XH, YN, XL, ZN, CORES), ALL)
    cls, ptl = ("xh", "y"), ("xl", "z", "core")
    placed = (P(cls, ptl, None), P(ALL, None), P(ALL), P(ALL), P(ALL), P(ALL))
    return jax.shard_map(
        body, mesh=fine, in_specs=placed, out_specs=P(cls, ptl), check_vma=False
    )
```
